512 devices in a mesh: probe: 8 (over y_lo, core), space: 64 (over y_hi, x, z).
Axes of the slice: x: 4, y: 8 (y_hi: 2, y_lo: 4; y = y_hi * 4 + y_lo), z: 8, core: 2. Of those that a mesh axis runs over, the one named last changes fastest.
Arguments:
- probe_dirs: float32 [32, 64, 256], P('probe', 'space'), may hold values from -6 to 6
- log_param: float32 [64, 256], P('space'), may hold values from -1 to 1
- background: float32 [512, 32, 512], P('space'), may hold values from 0.3 to 1.5
- site_class: int32 [512, 32, 512], P('space'), may hold values from 0 to 3
- trap_density: float32 [4], replicated, may hold values from 0.2 to 1
Outputs:
- q_basis: float32 [32, 64, 256], P('probe', 'space')
- lower_factor: float32 [32, 32], replicated
The draws below stay inside these ranges and needn't reach their ends.
All inputs are finite; a program needn't handle non-finite values.
Results may differ from the reference program's by a relative error of at most 0.0003.
Values sent between devices are 32-bit elements; how exact they have to be, the bound alone decides.
A program may use at most 64 MiB of HBM per device.

```python
import math
import jax
import jax.numpy as jnp
from jax import lax

PX = 64
PY = 4
REF = 8
NCLASS = 4
STEPS = 4
PROBES = 32
PZ = 64
PCELLS = 256
NZ = 512
NFY = 32
NFX = 512
NCOARSE = 16384


def draw_probe_dirs(key, part):
    group_count = max(1, PROBES // 4)
    key_base = jax.random.fold_in(key, 101)
    key_noise = jax.random.fold_in(key, 202)
    key_gain = jax.random.fold_in(key, 303)
    bases = jnp.clip(jax.random.normal(key_base, (group_count, PZ, PCELLS), jnp.float32), -4.0, 4.0)
    noise = jnp.clip(jax.random.normal(key_noise, (PROBES, PZ, PCELLS), jnp.float32), -4.0, 4.0)
    spread = 1.0 / 128.0
    gains = jnp.exp(jax.random.uniform(key_gain, (PROBES,), jnp.float32, -0.35, 0.35))
    member = jnp.arange(PROBES, dtype=jnp.int32) % group_count
    chosen = bases[member]
    return chosen * gains[:, None, None] + spread * noise


def set_ends(values, own_key, smallest, high):
    dims = values.shape
    place = [jax.random.randint(jax.random.fold_in(own_key, axis), (), 0, dims[axis]) for axis in range(len(dims))]
    values = values.at[tuple(place)].set(smallest)
    longest = dims.index(max(dims))
    place[longest] = (place[longest] + 1) % dims[longest]
    return values.at[tuple(place)].set(high)


def shard_levels(key, dims, split, low, high):
    level, own = 1.0, jax.random.fold_in(key, 6)
    for axis_at, blocks in split:
        steps = jnp.exp(jax.random.uniform(jax.random.fold_in(own, axis_at), (blocks,), jnp.float32, low / len(split), high / len(split)))
        level = level * jnp.repeat(steps, dims[axis_at] // blocks).reshape([-1 if axis == axis_at else 1 for axis in range(len(dims))])
    return level


def setup_inputs(seed: int = 0) -> dict:
    key_of = jax.random.split(jax.random.key(seed), 6)
    return {
        "probe_dirs": draw_probe_dirs(jax.random.fold_in(key_of[5], 71), 0),
        "log_param": jnp.clip(jax.random.uniform(key_of[1], (PZ, PCELLS), jnp.float32, -1.0, 1.0) * shard_levels(key_of[1], (PZ, PCELLS), ((0, 64),), -0.4, 0.0), -1.0, 1.0),
        "background": jnp.clip(0.3 + 1.2 * jax.random.uniform(key_of[2], (NZ, NFY, NFX), jnp.float32) ** shard_levels(key_of[2], (NZ, NFY, NFX), ((0, 64),), -0.2, 0.2), 0.3, 1.5),
        "site_class": set_ends(jax.random.randint(key_of[3], (NZ, NFY, NFX), 0, NCLASS), jax.random.fold_in(key_of[3], 1), 0, NCLASS - 1).astype(jnp.int32),
        "trap_density": jnp.clip(jnp.exp(jax.random.uniform(key_of[4], (NCLASS,), jnp.float32, math.log(0.2), math.log(1.0))), 0.2, 1.0),
    }


TIME_STEP = 0.12

def lower_solve(factor, rows):
    return lax.linalg.triangular_solve(factor, rows, left_side=True, lower=True)

def prolong(coarse):
    leading = coarse.shape[:-2]
    planes = coarse.shape[-2]
    coarse_grid = coarse.reshape(leading + (planes, PY, PX))
    expanded = jnp.broadcast_to(coarse_grid[..., :, None, :, None, :, None], leading + (planes, REF, PY, REF, PX, REF))
    return expanded.reshape(leading + (planes * REF, PY * REF, PX * REF))

def restrict(finegrid):
    planes = finegrid.shape[0] // REF
    shaped = finegrid.reshape((planes, REF, PY, REF, PX, REF))
    return jnp.sum(shaped, axis=(1, 3, 5)).reshape((planes, PY * PX))

def stencil(padded, current, trap_rate):
    up_down = padded[2:, :, :] + padded[:-2, :, :]
    flat_pad = jnp.pad(current, ((0, 0), (1, 1), (1, 1)))
    lateral = flat_pad[:, 2:, 1:-1] + flat_pad[:, :-2, 1:-1] + flat_pad[:, 1:-1, 2:] + flat_pad[:, 1:-1, :-2]
    return current + TIME_STEP * (up_down + lateral - 6.0 * current - trap_rate * current)

def advance(current, trap_rate):
    padded = jnp.pad(current, ((1, 1), (0, 0), (0, 0)))
    return stencil(padded, current, trap_rate)

def reference(probe_dirs, log_param, background, site_class, trap_density):
    trap_rate = trap_density[site_class] * jnp.exp(prolong(log_param))
    source = -TIME_STEP * trap_rate * background

    def hessian_column(direction):
        tangent = source * prolong(direction)
        for step_index in range(STEPS - 1):
            tangent = advance(tangent, trap_rate)
        adjoint = tangent
        summed = adjoint
        for step_index in range(STEPS - 1):
            adjoint = advance(adjoint, trap_rate)
            summed = summed + adjoint
        return restrict(source * summed)
    images = lax.map(hessian_column, probe_dirs)
    rows = images.reshape((PROBES, NCOARSE))
    highest = lax.Precision.HIGHEST
    gram_one = jnp.dot(rows.astype(jnp.float32), rows.T.astype(jnp.float32), precision=highest, preferred_element_type=jnp.float32) / NCOARSE
    factor_one = jnp.linalg.cholesky(gram_one)
    basis_one = lower_solve(factor_one, rows)
    gram_two = jnp.dot(basis_one.astype(jnp.float32), basis_one.T.astype(jnp.float32), precision=highest, preferred_element_type=jnp.float32) / NCOARSE
    factor_two = jnp.linalg.cholesky(gram_two)
    q_rows = lower_solve(factor_two, basis_one)
    lower_factor = jnp.dot(factor_one.astype(jnp.float32), factor_two.astype(jnp.float32), precision=highest, preferred_element_type=jnp.float32)
    return (q_rows.reshape((PROBES, PZ, PCELLS)), lower_factor)
```

```python
import jax
import jax.numpy as jnp
from jax import lax
from jax.sharding import PartitionSpec as P

PX = 64
PY = 4
REF = 8
STEPS = 4


TIME_STEP = 0.12


def padded_2(x, sides, width):
    for axis, dim in sides:
        count, length = (lax.axis_size(axis), x.shape[dim])
        up = [(i, (i + 1) % count) for i in range(count - 1)]
        down = [(j, i) for i, j in up]
        last = lax.slice_in_dim(x, length - width, length, axis=dim)
        first = lax.slice_in_dim(x, 0, width, axis=dim)
        before = lax.ppermute(last, axis, up)
        after = lax.ppermute(first, axis, down)
        x = jnp.concatenate([before, x, after], axis=dim)
    return x


def lower_solve(factor, rows):
    return lax.linalg.triangular_solve(factor, rows, left_side=True, lower=True)


def prolong(coarse):
    leading = coarse.shape[:-2]
    planes = coarse.shape[-2]
    coarse_grid = coarse.reshape(leading + (planes, PY, PX))
    expanded = jnp.broadcast_to(
        coarse_grid[..., :, None, :, None, :, None], leading + (planes, REF, PY, REF, PX, REF)
    )
    return expanded.reshape(leading + (planes * REF, PY * REF, PX * REF))


def restrict(finegrid):
    probe_count = finegrid.shape[0]
    planes = finegrid.shape[1] // REF
    shaped = finegrid.reshape((probe_count, planes, REF, PY, REF, PX, REF))
    return jnp.sum(shaped, axis=(2, 4, 6)).reshape((probe_count, planes, PY * PX))


def stencil(padded, current, trap_rate):
    up_down = padded[:, 2:, :, :] + padded[:, :-2, :, :]
    flat_pad = jnp.pad(current, ((0, 0), (0, 0), (1, 1), (1, 1)))
    lateral = (
        flat_pad[:, :, 2:, 1:-1]
        + flat_pad[:, :, :-2, 1:-1]
        + flat_pad[:, :, 1:-1, 2:]
        + flat_pad[:, :, 1:-1, :-2]
    )
    return current + TIME_STEP * (up_down + lateral - 6.0 * current - trap_rate[None] * current)


def cholesky_pass(rows, gram_sum, cell_count):
    highest = lax.Precision.HIGHEST
    partial_gram = jnp.dot(rows, rows.T, precision=highest, preferred_element_type=jnp.float32)
    gram_matrix = gram_sum(partial_gram) / cell_count
    factor = jnp.linalg.cholesky(gram_matrix)
    return (lower_solve(factor, rows), factor)


def shards(probe_dirs, log_param, background, site_class, trap_density):
    probe_count = probe_dirs.shape[0]
    planes = probe_dirs.shape[1]
    plane_cells = probe_dirs.shape[2]
    density = jnp.zeros(site_class.shape, jnp.float32)
    for class_index in range(trap_density.shape[0]):
        density = density + jnp.where(site_class == class_index, trap_density[class_index], 0.0)
    trap_rate = density * jnp.exp(prolong(log_param))
    source = -TIME_STEP * trap_rate * background
    tangent = source[None] * prolong(probe_dirs)
    for step_index in range(STEPS - 1):
        padded = padded_2(tangent, (("space", 1),), 1)
        tangent = stencil(padded, tangent, trap_rate)
    adjoint = tangent
    summed = adjoint
    for step_index in range(STEPS - 1):
        padded = padded_2(adjoint, (("space", 1),), 1)
        adjoint = stencil(padded, adjoint, trap_rate)
        summed = summed + adjoint
    images = restrict(source[None] * summed).reshape((probe_count, planes * plane_cells))
    cell_count = float(planes * lax.axis_size("space") * plane_cells)
    highest = lax.Precision.HIGHEST
    every_probe = lax.all_gather(images, "probe", axis=0, tiled=True)

    def space_sum(partial_gram):
        count = lax.axis_size("space")
        distance = 1
        while distance < count:
            swap = [(i, i ^ distance) for i in range(count)]
            partial_gram = partial_gram + lax.ppermute(partial_gram, "space", swap)
            distance *= 2
        return partial_gram

    basis_one, factor_one = cholesky_pass(every_probe, space_sum, cell_count)
    q_rows, factor_two = cholesky_pass(basis_one, space_sum, cell_count)
    q_local = lax.dynamic_slice_in_dim(
        q_rows, lax.axis_index("probe") * probe_count, probe_count, 0
    )
    lower_factor = jnp.dot(
        factor_one, factor_two, precision=highest, preferred_element_type=jnp.float32
    )
    return (q_local.reshape((probe_count, planes, plane_cells)), lower_factor)


def solution(mesh):
    placed = (
        P("probe", "space", None),
        P("space", None),
        P("space", None, None),
        P("space", None, None),
        P(),
    )
    return jax.shard_map(
        shards,
        mesh=mesh,
        in_specs=placed,
        out_specs=(P("probe", "space", None), P()),
        check_vma=False,
    )
```

```python
import jax
import jax.numpy as jnp
from jax import lax
from jax.experimental import pallas as pl
from jax.experimental.pallas import tpu as pltpu
from jax.sharding import PartitionSpec as P

PX = 64
PY = 4
REF = 8
STEPS = 4


TIME_STEP = 0.12


def padded_2(x, sides, width):
    for axis, dim in sides:
        count, length = (lax.axis_size(axis), x.shape[dim])
        up = [(i, (i + 1) % count) for i in range(count - 1)]
        down = [(j, i) for i, j in up]
        last = lax.slice_in_dim(x, length - width, length, axis=dim)
        first = lax.slice_in_dim(x, 0, width, axis=dim)
        before = lax.ppermute(last, axis, up)
        after = lax.ppermute(first, axis, down)
        x = jnp.concatenate([before, x, after], axis=dim)
    return x


def prolong(coarse):
    leading = coarse.shape[:-2]
    planes = coarse.shape[-2]
    coarse_grid = coarse.reshape(leading + (planes, PY, PX))
    expanded = jnp.broadcast_to(
        coarse_grid[..., :, None, :, None, :, None], leading + (planes, REF, PY, REF, PX, REF)
    )
    return expanded.reshape(leading + (planes * REF, PY * REF, PX * REF))


def restrict(finegrid):
    probe_count = finegrid.shape[0]
    planes = finegrid.shape[1] // REF
    shaped = finegrid.reshape((probe_count, planes, REF, PY, REF, PX, REF))
    return jnp.sum(shaped, axis=(2, 4, 6)).reshape((probe_count, planes, PY * PX))


def stencil(padded, current, trap_rate):
    up_down = padded[:, 2:, :, :] + padded[:, :-2, :, :]
    flat_pad = jnp.pad(current, ((0, 0), (0, 0), (1, 1), (1, 1)))
    lateral = (
        flat_pad[:, :, 2:, 1:-1]
        + flat_pad[:, :, :-2, 1:-1]
        + flat_pad[:, :, 1:-1, 2:]
        + flat_pad[:, :, 1:-1, :-2]
    )
    return current + TIME_STEP * (up_down + lateral - 6.0 * current - trap_rate[None] * current)


def dot_highest(a, b, contract):
    return lax.dot_general(
        a, b, (contract, ((), ())), precision=lax.Precision.HIGHEST,
        preferred_element_type=jnp.float32,
    )


def factor_and_inverse(gram):
    n = gram.shape[0]
    row_at = lax.broadcasted_iota(jnp.int32, (n, 2 * n), 0)
    lane_at = lax.broadcasted_iota(jnp.int32, (n, 2 * n), 1)
    factor_row = lax.broadcasted_iota(jnp.int32, (n, n), 0)
    factor_lane = lax.broadcasted_iota(jnp.int32, (n, n), 1)
    work = jnp.concatenate([gram, jnp.zeros((n, n), jnp.float32)], axis=1)
    work = work + jnp.where(lane_at == row_at + n, 1.0, 0.0)
    factor = jnp.zeros((n, n), jnp.float32)
    for j in range(n):
        scale = lax.rsqrt(work[j : j + 1, j : j + 1])
        row = work[j : j + 1, :] * scale
        column = work[:, j : j + 1] * scale
        keep = (factor_lane == j) & (factor_row >= j)
        factor = jnp.where(keep, jnp.broadcast_to(column, (n, n)), factor)
        work = jnp.where(
            row_at > j, work - column * row, jnp.where(row_at == j, row, work)
        )
    return factor, work[:, n:]


GROUP = 8


def orthogonalize_kernel(
    cell_count, images_ref, q_ref, lower_ref, gathered, rows, grams, image_send, image_recv,
    gram_send, gram_recv,
):
    mesh_id = pl.DeviceIdType.MESH
    me = lax.axis_index("probe")
    place = lax.axis_index("space")
    inner, outer = lax.rem(place, GROUP), lax.div(place, GROUP)

    def probe_peer(k):
        return {"probe": lax.rem(me + k, GROUP)}

    def inner_peer(k):
        return {"space": outer * GROUP + lax.rem(inner + k, GROUP)}

    def outer_peer(k):
        return {"space": lax.rem(outer + k, GROUP) * GROUP + inner}

    barrier = pltpu.get_barrier_semaphore()
    for peer in (probe_peer, inner_peer, outer_peer):
        for k in range(1, GROUP):
            pl.semaphore_signal(barrier, inc=1, device_id=peer(k), device_id_type=mesh_id)
    pl.semaphore_wait(barrier, 3 * (GROUP - 1))

    def send(src, dst, send_sem, recv_sem, device):
        return pltpu.make_async_remote_copy(
            src_ref=src, dst_ref=dst, send_sem=send_sem, recv_sem=recv_sem,
            device_id=device, device_id_type=mesh_id,
        )

    copies = []
    for k in range(1, GROUP):
        copy = send(
            images_ref, gathered.at[me], image_send.at[k], image_recv.at[me], probe_peer(k)
        )
        copy.start()
        copies.append(copy)
    gathered[me] = images_ref[...]
    for k in range(1, GROUP):
        slot = lax.rem(me + k, GROUP)
        send(
            images_ref, gathered.at[slot], image_send.at[k], image_recv.at[slot], probe_peer(k)
        ).wait_recv()
    count = images_ref.shape[0]
    for slot in range(GROUP):
        rows[slot * count : (slot + 1) * count, :] = gathered[slot]

    def group_sum(value, stage, mine, peer):
        box = grams.at[stage]
        box[mine] = value
        for k in range(1, GROUP):
            copy = send(
                box.at[mine], box.at[mine], gram_send.at[stage, k], gram_recv.at[stage, mine],
                peer(k),
            )
            copy.start()
            copies.append(copy)
        for k in range(1, GROUP):
            slot = lax.rem(mine + k, GROUP)
            send(
                box.at[slot], box.at[slot], gram_send.at[stage, k], gram_recv.at[stage, slot],
                peer(k),
            ).wait_recv()
        total = box[0]
        for slot in range(1, GROUP):
            total = total + box[slot]
        return total

    def space_gram(basis, stage):
        gram = dot_highest(basis, basis, ((1,), (1,)))
        gram = group_sum(gram, stage, inner, inner_peer)
        gram = group_sum(gram, stage + 1, outer, outer_peer)
        return gram * (1.0 / cell_count)

    images = rows[...]
    factor_one, inverse_one = factor_and_inverse(space_gram(images, 0))
    basis_one = dot_highest(inverse_one, images, ((1,), (0,)))
    factor_two, inverse_two = factor_and_inverse(space_gram(basis_one, 2))
    q_rows = dot_highest(inverse_two, basis_one, ((1,), (0,)))
    for slot in range(GROUP):
        gathered[slot] = q_rows[slot * count : (slot + 1) * count, :]
    q_ref[...] = gathered[me]
    lower_ref[...] = dot_highest(factor_one, factor_two, ((1,), (0,)))
    for copy in copies:
        copy.wait_send()


def orthogonalize(images, cell_count):
    count, cells = images.shape
    probes = count * GROUP
    vmem = pl.BlockSpec(memory_space=pltpu.VMEM)

    def body(*refs):
        orthogonalize_kernel(cell_count, *refs)

    return pl.pallas_call(
        body,
        out_shape=(
            jax.ShapeDtypeStruct((count, cells), jnp.float32),
            jax.ShapeDtypeStruct((probes, probes), jnp.float32),
        ),
        in_specs=[vmem],
        out_specs=(vmem, vmem),
        scratch_shapes=[
            pltpu.VMEM((GROUP, count, cells), jnp.float32),
            pltpu.VMEM((probes, cells), jnp.float32),
            pltpu.VMEM((4, GROUP, probes, probes), jnp.float32),
            pltpu.SemaphoreType.DMA((GROUP,)),
            pltpu.SemaphoreType.DMA((GROUP,)),
            pltpu.SemaphoreType.DMA((4, GROUP)),
            pltpu.SemaphoreType.DMA((4, GROUP)),
        ],
        compiler_params=pltpu.CompilerParams(collective_id=0, has_side_effects=True),
    )(images)


def shards(probe_dirs, log_param, background, site_class, trap_density):
    probe_count = probe_dirs.shape[0]
    planes = probe_dirs.shape[1]
    plane_cells = probe_dirs.shape[2]
    density = jnp.zeros(site_class.shape, jnp.float32)
    for class_index in range(trap_density.shape[0]):
        density = density + jnp.where(site_class == class_index, trap_density[class_index], 0.0)
    trap_rate = density * jnp.exp(prolong(log_param))
    source = -TIME_STEP * trap_rate * background
    tangent = source[None] * prolong(probe_dirs)
    for step_index in range(STEPS - 1):
        padded = padded_2(tangent, (("space", 1),), 1)
        tangent = stencil(padded, tangent, trap_rate)
    adjoint = tangent
    summed = adjoint
    for step_index in range(STEPS - 1):
        padded = padded_2(adjoint, (("space", 1),), 1)
        adjoint = stencil(padded, adjoint, trap_rate)
        summed = summed + adjoint
    images = restrict(source[None] * summed).reshape((probe_count, planes * plane_cells))
    cell_count = float(planes * lax.axis_size("space") * plane_cells)
    q_local, lower_factor = orthogonalize(images, cell_count)
    return (q_local.reshape((probe_count, planes, plane_cells)), lower_factor)


def solution(mesh):
    placed = (
        P("probe", "space", None),
        P("space", None),
        P("space", None, None),
        P("space", None, None),
        P(),
    )
    return jax.shard_map(
        shards,
        mesh=mesh,
        in_specs=placed,
        out_specs=(P("probe", "space", None), P()),
        check_vma=False,
    )
```

```python
import jax
import jax.numpy as jnp
from jax import lax
from jax.experimental import pallas as pl
from jax.experimental.pallas import tpu as pltpu
from jax.sharding import PartitionSpec as P

PX = 64
PY = 4
REF = 8
STEPS = 4


TIME_STEP = 0.12


def prolong(coarse):
    leading = coarse.shape[:-2]
    planes = coarse.shape[-2]
    coarse_grid = coarse.reshape(leading + (planes, PY, PX))
    expanded = jnp.broadcast_to(
        coarse_grid[..., :, None, :, None, :, None], leading + (planes, REF, PY, REF, PX, REF)
    )
    return expanded.reshape(leading + (planes * REF, PY * REF, PX * REF))


def dot_highest(a, b, contract):
    return lax.dot_general(
        a, b, (contract, ((), ())), precision=lax.Precision.HIGHEST,
        preferred_element_type=jnp.float32,
    )


def factor_and_inverse(gram):
    n = gram.shape[0]
    row_at = lax.broadcasted_iota(jnp.int32, (n, 2 * n), 0)
    lane_at = lax.broadcasted_iota(jnp.int32, (n, 2 * n), 1)
    factor_row = lax.broadcasted_iota(jnp.int32, (n, n), 0)
    factor_lane = lax.broadcasted_iota(jnp.int32, (n, n), 1)
    work = jnp.concatenate([gram, jnp.zeros((n, n), jnp.float32)], axis=1)
    work = work + jnp.where(lane_at == row_at + n, 1.0, 0.0)
    factor = jnp.zeros((n, n), jnp.float32)
    for j in range(n):
        scale = lax.rsqrt(work[j : j + 1, j : j + 1])
        row = work[j : j + 1, :] * scale
        column = work[:, j : j + 1] * scale
        keep = (factor_lane == j) & (factor_row >= j)
        factor = jnp.where(keep, jnp.broadcast_to(column, (n, n)), factor)
        work = jnp.where(
            row_at > j, work - column * row, jnp.where(row_at == j, row, work)
        )
    return factor, work[:, n:]


GROUP = 8


def orthogonalize_kernel(
    cell_count, images_ref, q_ref, lower_ref, gathered, rows, grams, image_send, image_recv,
    gram_send, gram_recv,
):
    mesh_id = pl.DeviceIdType.MESH
    me = lax.axis_index("probe")
    place = lax.axis_index("space")
    inner, outer = lax.rem(place, GROUP), lax.div(place, GROUP)

    def probe_peer(k):
        return {"probe": lax.rem(me + k, GROUP)}

    def inner_peer(k):
        return {"space": outer * GROUP + lax.rem(inner + k, GROUP)}

    def outer_peer(k):
        return {"space": lax.rem(outer + k, GROUP) * GROUP + inner}

    barrier = pltpu.get_barrier_semaphore()
    for peer in (probe_peer, inner_peer, outer_peer):
        for k in range(1, GROUP):
            pl.semaphore_signal(barrier, inc=1, device_id=peer(k), device_id_type=mesh_id)
    pl.semaphore_wait(barrier, 3 * (GROUP - 1))

    def send(src, dst, send_sem, recv_sem, device):
        return pltpu.make_async_remote_copy(
            src_ref=src, dst_ref=dst, send_sem=send_sem, recv_sem=recv_sem,
            device_id=device, device_id_type=mesh_id,
        )

    copies = []
    for k in range(1, GROUP):
        copy = send(
            images_ref, gathered.at[me], image_send.at[k], image_recv.at[me], probe_peer(k)
        )
        copy.start()
        copies.append(copy)
    gathered[me] = images_ref[...]
    for k in range(1, GROUP):
        slot = lax.rem(me + k, GROUP)
        send(
            images_ref, gathered.at[slot], image_send.at[k], image_recv.at[slot], probe_peer(k)
        ).wait_recv()
    count = images_ref.shape[0]
    for slot in range(GROUP):
        rows[slot * count : (slot + 1) * count, :] = gathered[slot]

    def group_sum(value, stage, mine, peer):
        box = grams.at[stage]
        box[mine] = value
        for k in range(1, GROUP):
            copy = send(
                box.at[mine], box.at[mine], gram_send.at[stage, k], gram_recv.at[stage, mine],
                peer(k),
            )
            copy.start()
            copies.append(copy)
        for k in range(1, GROUP):
            slot = lax.rem(mine + k, GROUP)
            send(
                box.at[slot], box.at[slot], gram_send.at[stage, k], gram_recv.at[stage, slot],
                peer(k),
            ).wait_recv()
        total = box[0]
        for slot in range(1, GROUP):
            total = total + box[slot]
        return total

    def space_gram(basis, stage):
        gram = dot_highest(basis, basis, ((1,), (1,)))
        gram = group_sum(gram, stage, inner, inner_peer)
        gram = group_sum(gram, stage + 1, outer, outer_peer)
        return gram * (1.0 / cell_count)

    images = rows[...]
    factor_one, inverse_one = factor_and_inverse(space_gram(images, 0))
    basis_one = dot_highest(inverse_one, images, ((1,), (0,)))
    factor_two, inverse_two = factor_and_inverse(space_gram(basis_one, 2))
    q_rows = dot_highest(inverse_two, basis_one, ((1,), (0,)))
    for slot in range(GROUP):
        gathered[slot] = q_rows[slot * count : (slot + 1) * count, :]
    q_ref[...] = gathered[me]
    lower_ref[...] = dot_highest(factor_one, factor_two, ((1,), (0,)))
    for copy in copies:
        copy.wait_send()


def orthogonalize(images, cell_count):
    count, cells = images.shape
    probes = count * GROUP
    vmem = pl.BlockSpec(memory_space=pltpu.VMEM)

    def body(*refs):
        orthogonalize_kernel(cell_count, *refs)

    return pl.pallas_call(
        body,
        out_shape=(
            jax.ShapeDtypeStruct((count, cells), jnp.float32),
            jax.ShapeDtypeStruct((probes, probes), jnp.float32),
        ),
        in_specs=[vmem],
        out_specs=(vmem, vmem),
        scratch_shapes=[
            pltpu.VMEM((GROUP, count, cells), jnp.float32),
            pltpu.VMEM((probes, cells), jnp.float32),
            pltpu.VMEM((4, GROUP, probes, probes), jnp.float32),
            pltpu.SemaphoreType.DMA((GROUP,)),
            pltpu.SemaphoreType.DMA((GROUP,)),
            pltpu.SemaphoreType.DMA((4, GROUP)),
            pltpu.SemaphoreType.DMA((4, GROUP)),
        ],
        compiler_params=pltpu.CompilerParams(collective_id=0, has_side_effects=True),
    )(images)


REACH = 2 * (STEPS - 1)
EXTENDED = REF + 2 * REACH
CHUNK = 16


def window_kernel(
    edge_ref, trap_ref, source_ref, halo_ref, dirs_ref, images_ref, keep, source, first, second,
    summed,
):
    fine_y, fine_x = PY * REF, PX * REF
    share = halo_ref.shape[2] // CHUNK
    own = slice(REACH, REACH + REF)
    keep[own] = (1.0 - 6.0 * TIME_STEP) - TIME_STEP * trap_ref[...]
    source[own] = source_ref[...]
    for side in range(2):
        base = side * (REACH + REF)
        inside = edge_ref[side]
        for plane in range(REACH):
            for half in range(fine_y // CHUNK):
                rows = slice(half * CHUNK, (half + 1) * CHUNK)

                def piece(at):
                    chunk = at * (fine_y // CHUNK) + half
                    start = (chunk % share) * CHUNK
                    return halo_ref[chunk // share, side, start : start + CHUNK, :]

                trap = piece(plane)
                keep[base + plane, rows, :] = inside * (
                    (1.0 - 6.0 * TIME_STEP) - TIME_STEP * trap
                )
                source[base + plane, rows, :] = inside * piece(REACH + plane)

    x_fine = lax.broadcasted_iota(jnp.int32, (PX, fine_x), 1)
    x_cell = lax.broadcasted_iota(jnp.int32, (PX, fine_x), 0)
    spread_x = jnp.where(x_fine // REF == x_cell, 1.0, 0.0)
    y_fine = lax.broadcasted_iota(jnp.int32, (fine_y, PY), 0)
    y_cell = lax.broadcasted_iota(jnp.int32, (fine_y, PY), 1)
    spread_y = jnp.where(y_fine // REF == y_cell, 1.0, 0.0)
    row_at = lax.broadcasted_iota(jnp.int32, (fine_y, fine_x), 0)
    lane_at = lax.broadcasted_iota(jnp.int32, (fine_y, fine_x), 1)

    def advance(src, dst, low, high, add):
        def plane_step(i, carry):
            below = (i >= REACH).astype(jnp.float32)
            above = (i < REACH + REF).astype(jnp.float32)
            weight = TIME_STEP * (below + (1.0 - below) * edge_ref[0])
            weight = weight * (above + (1.0 - above) * edge_ref[1])
            v = src[i]
            around = src[i - 1] + src[i + 1]
            around += jnp.where(row_at == 0, 0.0, pltpu.roll(v, 1, 0))
            around += jnp.where(row_at == fine_y - 1, 0.0, pltpu.roll(v, fine_y - 1, 0))
            around += jnp.where(lane_at == 0, 0.0, pltpu.roll(v, 1, 1))
            around += jnp.where(lane_at == fine_x - 1, 0.0, pltpu.roll(v, fine_x - 1, 1))
            new = keep[i] * v + weight * around
            dst[i] = new
            if add:
                @pl.when((i >= REACH) & (i < REACH + REF))
                def _():
                    at = i - REACH
                    summed[at] = summed[at] + new
            return carry

        lax.fori_loop(low, high, plane_step, 0)

    def probe_step(p, carry):
        for cell in range(3):
            coarse = dirs_ref[p, cell]
            wide = dot_highest(coarse, spread_x, ((1,), (0,)))
            fine = dot_highest(spread_y, wide, ((1,), (0,)))
            low = max(0, REACH - REF + cell * REF)
            high = min(EXTENDED, REACH + cell * REF)
            for i in range(low, high):
                first[i] = source[i] * fine
        bufs = (first, second)
        for n in range(1, 2 * STEPS - 1):
            src, dst = bufs[(n - 1) % 2], bufs[n % 2]
            advance(src, dst, n, EXTENDED - n, n >= STEPS)
            if n == STEPS - 1:
                summed[...] = dst[own]
        total = source[REACH] * summed[0]
        for at in range(1, REF):
            total = total + source[REACH + at] * summed[at]
        narrow = dot_highest(total, spread_x, ((1,), (1,)))
        images_ref[p] = dot_highest(spread_y, narrow, ((0,), (0,)))
        return carry

    lax.fori_loop(0, dirs_ref.shape[0], probe_step, 0)


def window_images(edge, trap_rate, source, halo, dirs):
    vmem = pl.BlockSpec(memory_space=pltpu.VMEM)
    plane = (PY * REF, PX * REF)
    return pl.pallas_call(
        window_kernel,
        out_shape=jax.ShapeDtypeStruct((dirs.shape[0], PY, PX), jnp.float32),
        in_specs=[pl.BlockSpec(memory_space=pltpu.SMEM)] + [vmem] * 4,
        out_specs=vmem,
        scratch_shapes=[
            pltpu.VMEM((EXTENDED,) + plane, jnp.float32),
            pltpu.VMEM((EXTENDED,) + plane, jnp.float32),
            pltpu.VMEM((EXTENDED,) + plane, jnp.float32),
            pltpu.VMEM((EXTENDED,) + plane, jnp.float32),
            pltpu.VMEM((REF,) + plane, jnp.float32),
        ],
        compiler_params=pltpu.CompilerParams(vmem_limit_bytes=32 * 1024 * 1024),
    )(edge, trap_rate, source, halo, dirs)


def shards(probe_dirs, log_param, background, site_class, trap_density):
    probe_count, planes, plane_cells = probe_dirs.shape
    slabs, slab = lax.axis_size("space"), lax.axis_index("space")
    up = [(i, i + 1) for i in range(slabs - 1)]
    down = [(j, i) for i, j in up]
    density = jnp.zeros(site_class.shape, jnp.float32)
    for class_index in range(trap_density.shape[0]):
        density = density + jnp.where(site_class == class_index, trap_density[class_index], 0.0)
    trap_rate = density * prolong(jnp.exp(log_param))
    source = -TIME_STEP * trap_rate * background

    def my_share(part):
        both = jnp.concatenate([trap_rate[part], source[part]], axis=0)
        rows = both.reshape((-1, PX * REF))
        length = rows.shape[0] // lax.axis_size("probe")
        return lax.dynamic_slice_in_dim(rows, lax.axis_index("probe") * length, length, 0)

    from_below = lax.ppermute(my_share(slice(REF - REACH, REF)), "space", up)
    from_above = lax.ppermute(my_share(slice(0, REACH)), "space", down)
    halo = lax.all_gather(jnp.stack([from_below, from_above]), "probe", axis=0)
    dirs = jnp.concatenate(
        [
            lax.ppermute(probe_dirs, "space", up),
            probe_dirs,
            lax.ppermute(probe_dirs, "space", down),
        ],
        axis=1,
    ).reshape((probe_count, 3, PY, PX))
    edge = jnp.stack([slab > 0, slab < slabs - 1]).astype(jnp.float32)
    images = window_images(edge, trap_rate, source, halo, dirs)
    images = images.reshape((probe_count, planes * plane_cells))
    cell_count = float(planes * slabs * plane_cells)
    q_local, lower_factor = orthogonalize(images, cell_count)
    return (q_local.reshape((probe_count, planes, plane_cells)), lower_factor)


def solution(mesh):
    placed = (
        P("probe", "space", None),
        P("space", None),
        P("space", None, None),
        P("space", None, None),
        P(),
    )
    return jax.shard_map(
        shards,
        mesh=mesh,
        in_specs=placed,
        out_specs=(P("probe", "space", None), P()),
        check_vma=False,
    )
```

```python
import jax
import jax.numpy as jnp
from jax import lax
from jax.experimental import pallas as pl
from jax.experimental.pallas import tpu as pltpu
from jax.sharding import PartitionSpec as P

PX = 64
PY = 4
REF = 8
STEPS = 4


TIME_STEP = 0.12


def prolong(coarse):
    leading = coarse.shape[:-2]
    planes = coarse.shape[-2]
    coarse_grid = coarse.reshape(leading + (planes, PY, PX))
    expanded = jnp.broadcast_to(
        coarse_grid[..., :, None, :, None, :, None], leading + (planes, REF, PY, REF, PX, REF)
    )
    return expanded.reshape(leading + (planes * REF, PY * REF, PX * REF))


def dot_highest(a, b, contract):
    return lax.dot_general(
        a, b, (contract, ((), ())), precision=lax.Precision.HIGHEST,
        preferred_element_type=jnp.float32,
    )


def factor_and_inverse(gram):
    n = gram.shape[0]
    row_at = lax.broadcasted_iota(jnp.int32, (n, 2 * n), 0)
    lane_at = lax.broadcasted_iota(jnp.int32, (n, 2 * n), 1)
    factor_row = lax.broadcasted_iota(jnp.int32, (n, n), 0)
    factor_lane = lax.broadcasted_iota(jnp.int32, (n, n), 1)
    work = jnp.concatenate([gram, jnp.zeros((n, n), jnp.float32)], axis=1)
    work = work + jnp.where(lane_at == row_at + n, 1.0, 0.0)
    factor = jnp.zeros((n, n), jnp.float32)
    for j in range(n):
        scale = lax.rsqrt(work[j : j + 1, j : j + 1])
        row = work[j : j + 1, :] * scale
        column = work[:, j : j + 1] * scale
        keep = (factor_lane == j) & (factor_row >= j)
        factor = jnp.where(keep, jnp.broadcast_to(column, (n, n)), factor)
        work = jnp.where(
            row_at > j, work - column * row, jnp.where(row_at == j, row, work)
        )
    return factor, work[:, n:]


GROUP = 8


def orthogonalize_kernel(
    cell_count, images_ref, q_ref, lower_ref, gathered, rows, grams, image_send, image_recv,
    gram_send, gram_recv,
):
    mesh_id = pl.DeviceIdType.MESH
    me = lax.axis_index("probe")
    place = lax.axis_index("space")
    inner, outer = lax.rem(place, GROUP), lax.div(place, GROUP)

    def probe_peer(k):
        return {"probe": lax.rem(me + k, GROUP)}

    def inner_peer(k):
        return {"space": outer * GROUP + lax.rem(inner + k, GROUP)}

    def outer_peer(k):
        return {"space": lax.rem(outer + k, GROUP) * GROUP + inner}

    barrier = pltpu.get_barrier_semaphore()
    for peer in (probe_peer, inner_peer, outer_peer):
        for k in range(1, GROUP):
            pl.semaphore_signal(barrier, inc=1, device_id=peer(k), device_id_type=mesh_id)
    pl.semaphore_wait(barrier, 3 * (GROUP - 1))

    def send(src, dst, send_sem, recv_sem, device):
        return pltpu.make_async_remote_copy(
            src_ref=src, dst_ref=dst, send_sem=send_sem, recv_sem=recv_sem,
            device_id=device, device_id_type=mesh_id,
        )

    copies = []
    for k in range(1, GROUP):
        copy = send(
            images_ref, gathered.at[me], image_send.at[k], image_recv.at[me], probe_peer(k)
        )
        copy.start()
        copies.append(copy)
    gathered[me] = images_ref[...]
    for k in range(1, GROUP):
        slot = lax.rem(me + k, GROUP)
        send(
            images_ref, gathered.at[slot], image_send.at[k], image_recv.at[slot], probe_peer(k)
        ).wait_recv()
    count = images_ref.shape[0]
    for slot in range(GROUP):
        rows[slot * count : (slot + 1) * count, :] = gathered[slot]

    def group_sum(value, stage, mine, peer):
        box = grams.at[stage]
        box[mine] = value
        for k in range(1, GROUP):
            copy = send(
                box.at[mine], box.at[mine], gram_send.at[stage, k], gram_recv.at[stage, mine],
                peer(k),
            )
            copy.start()
            copies.append(copy)
        for k in range(1, GROUP):
            slot = lax.rem(mine + k, GROUP)
            send(
                box.at[slot], box.at[slot], gram_send.at[stage, k], gram_recv.at[stage, slot],
                peer(k),
            ).wait_recv()
        total = box[0]
        for slot in range(1, GROUP):
            total = total + box[slot]
        return total

    def space_gram(basis, stage):
        gram = dot_highest(basis, basis, ((1,), (1,)))
        gram = group_sum(gram, stage, inner, inner_peer)
        gram = group_sum(gram, stage + 1, outer, outer_peer)
        return gram * (1.0 / cell_count)

    images = rows[...]
    factor_one, inverse_one = factor_and_inverse(space_gram(images, 0))
    basis_one = dot_highest(inverse_one, images, ((1,), (0,)))
    factor_two, inverse_two = factor_and_inverse(space_gram(basis_one, 2))
    q_rows = dot_highest(inverse_two, basis_one, ((1,), (0,)))
    for slot in range(GROUP):
        gathered[slot] = q_rows[slot * count : (slot + 1) * count, :]
    q_ref[...] = gathered[me]
    lower_ref[...] = dot_highest(factor_one, factor_two, ((1,), (0,)))
    for copy in copies:
        copy.wait_send()


def orthogonalize(images, cell_count):
    count, cells = images.shape
    probes = count * GROUP
    vmem = pl.BlockSpec(memory_space=pltpu.VMEM)

    def body(*refs):
        orthogonalize_kernel(cell_count, *refs)

    return pl.pallas_call(
        body,
        out_shape=(
            jax.ShapeDtypeStruct((count, cells), jnp.float32),
            jax.ShapeDtypeStruct((probes, probes), jnp.float32),
        ),
        in_specs=[vmem],
        out_specs=(vmem, vmem),
        scratch_shapes=[
            pltpu.VMEM((GROUP, count, cells), jnp.float32),
            pltpu.VMEM((probes, cells), jnp.float32),
            pltpu.VMEM((4, GROUP, probes, probes), jnp.float32),
            pltpu.SemaphoreType.DMA((GROUP,)),
            pltpu.SemaphoreType.DMA((GROUP,)),
            pltpu.SemaphoreType.DMA((4, GROUP)),
            pltpu.SemaphoreType.DMA((4, GROUP)),
        ],
        compiler_params=pltpu.CompilerParams(collective_id=0, has_side_effects=True),
    )(images)


REACH = 2 * (STEPS - 1)
EXTENDED = REF + 2 * REACH
CHUNK = 16


def window_kernel(
    edge_ref, trap_ref, source_ref, halo_ref, dirs_ref, images_ref, keep, source, first, second,
    summed, wide, narrow,
):
    fine_y, fine_x = PY * REF, PX * REF
    share = halo_ref.shape[2] // CHUNK
    own = slice(REACH, REACH + REF)
    keep[own] = (1.0 - 6.0 * TIME_STEP) - TIME_STEP * trap_ref[...]
    source[own] = source_ref[...]
    for side in range(2):
        base = side * (REACH + REF)
        inside = edge_ref[side]
        for plane in range(REACH):
            for half in range(fine_y // CHUNK):
                rows = slice(half * CHUNK, (half + 1) * CHUNK)

                def piece(at):
                    chunk = at * (fine_y // CHUNK) + half
                    start = (chunk % share) * CHUNK
                    return halo_ref[chunk // share, side, start : start + CHUNK, :]

                trap = piece(plane)
                keep[base + plane, rows, :] = inside * (
                    (1.0 - 6.0 * TIME_STEP) - TIME_STEP * trap
                )
                source[base + plane, rows, :] = inside * piece(REACH + plane)

    x_fine = lax.broadcasted_iota(jnp.int32, (PX, fine_x), 1)
    x_cell = lax.broadcasted_iota(jnp.int32, (PX, fine_x), 0)
    spread_x = jnp.where(x_fine // REF == x_cell, 1.0, 0.0)
    probes = dirs_ref.shape[0]
    all_wide = dot_highest(dirs_ref[...].reshape((-1, PX)), spread_x, ((1,), (0,)))
    for at in range(3 * PY * probes):
        wide[at // PY, at % PY, :] = all_wide[at]
    row_at = lax.broadcasted_iota(jnp.int32, (fine_y, fine_x), 0)
    lane_at = lax.broadcasted_iota(jnp.int32, (fine_y, fine_x), 1)

    def advance(src, dst, low, high, add):
        def plane_step(i, carry):
            below = (i >= REACH).astype(jnp.float32)
            above = (i < REACH + REF).astype(jnp.float32)
            weight = TIME_STEP * (below + (1.0 - below) * edge_ref[0])
            weight = weight * (above + (1.0 - above) * edge_ref[1])
            v = src[i]
            around = src[i - 1] + src[i + 1]
            around += jnp.where(row_at == 0, 0.0, pltpu.roll(v, 1, 0))
            around += jnp.where(row_at == fine_y - 1, 0.0, pltpu.roll(v, fine_y - 1, 0))
            around += jnp.where(lane_at == 0, 0.0, pltpu.roll(v, 1, 1))
            around += jnp.where(lane_at == fine_x - 1, 0.0, pltpu.roll(v, fine_x - 1, 1))
            new = keep[i] * v + weight * around
            dst[i] = new
            if add:
                summed[i] = summed[i] + new
            return carry

        lax.fori_loop(low, high, plane_step, 0, unroll=2)

    def probe_step(p, carry):
        for cell in range(3):
            coarse = wide[3 * p + cell]
            fine = jnp.concatenate(
                [jnp.broadcast_to(coarse[y : y + 1], (REF, fine_x)) for y in range(PY)], axis=0
            )
            low = max(0, REACH - REF + cell * REF)
            high = min(EXTENDED, REACH + cell * REF)
            for i in range(low, high):
                first[i] = source[i] * fine
        bufs = (first, second)
        for n in range(1, 2 * STEPS - 1):
            src, dst = bufs[(n - 1) % 2], bufs[n % 2]
            advance(src, dst, n, EXTENDED - n, n >= STEPS)
            if n == STEPS - 1:
                summed[own] = dst[own]
        total = source[REACH] * summed[REACH]
        for at in range(REACH + 1, REACH + REF):
            total = total + source[at] * summed[at]
        for y in range(PY):
            narrow[p, y : y + 1, :] = jnp.sum(
                total[y * REF : (y + 1) * REF], axis=0, keepdims=True
            )
        return carry

    lax.fori_loop(0, probes, probe_step, 0)
    for p in range(probes):
        images_ref[p] = dot_highest(narrow[p], spread_x, ((1,), (1,)))


def window_images(edge, trap_rate, source, halo, dirs):
    vmem = pl.BlockSpec(memory_space=pltpu.VMEM)
    plane = (PY * REF, PX * REF)
    return pl.pallas_call(
        window_kernel,
        out_shape=jax.ShapeDtypeStruct((dirs.shape[0], PY, PX), jnp.float32),
        in_specs=[pl.BlockSpec(memory_space=pltpu.SMEM)] + [vmem] * 4,
        out_specs=vmem,
        scratch_shapes=[
            pltpu.VMEM((EXTENDED,) + plane, jnp.float32),
            pltpu.VMEM((EXTENDED,) + plane, jnp.float32),
            pltpu.VMEM((EXTENDED,) + plane, jnp.float32),
            pltpu.VMEM((EXTENDED,) + plane, jnp.float32),
            pltpu.VMEM((EXTENDED,) + plane, jnp.float32),
            pltpu.VMEM((3 * dirs.shape[0], PY, PX * REF), jnp.float32),
            pltpu.VMEM((dirs.shape[0], PY, PX * REF), jnp.float32),
        ],
        compiler_params=pltpu.CompilerParams(vmem_limit_bytes=32 * 1024 * 1024),
    )(edge, trap_rate, source, halo, dirs)


CHIPS = 4


def halo_kernel(
    up_ref, down_ref, halo_ref, cross_send, cross_recv, line_send, line_recv, pair_send, pair_recv
):
    mesh_id = pl.DeviceIdType.MESH
    me = lax.axis_index("probe")
    slab, slabs = lax.axis_index("space"), lax.axis_size("space")
    core, chip = lax.rem(me, 2), lax.div(me, 2)
    partner = {"probe": chip * 2 + 1 - core}
    has_below, has_above = slab > 0, slab < slabs - 1

    def line_slot(k):
        return lax.rem(chip + k, CHIPS) * 2 + core

    barrier = pltpu.get_barrier_semaphore()

    def greet(device):
        pl.semaphore_signal(barrier, inc=1, device_id=device, device_id_type=mesh_id)

    for k in range(1, CHIPS):
        greet({"probe": line_slot(k)})
    greet(partner)

    @pl.when(has_below)
    def _():
        greet({"space": slab - 1})

    @pl.when(has_above)
    def _():
        greet({"space": slab + 1})

    pl.semaphore_wait(
        barrier, CHIPS + has_below.astype(jnp.int32) + has_above.astype(jnp.int32)
    )

    def send(src, dst, send_sem, recv_sem, device):
        return pltpu.make_async_remote_copy(
            src_ref=src, dst_ref=dst, send_sem=send_sem, recv_sem=recv_sem,
            device_id=device, device_id_type=mesh_id,
        )

    def cross(side):
        share, step = ((up_ref, 1), (down_ref, -1))[side]
        return send(
            share, halo_ref.at[me, side], cross_send.at[side], cross_recv.at[side],
            {"space": slab + step},
        )

    goes, comes = (has_above, has_below), (has_below, has_above)
    for side in range(2):

        @pl.when(goes[side])
        def _():
            cross(side).start()

    def line(side, slot, k):
        return send(
            halo_ref.at[slot, side], halo_ref.at[slot, side], line_send.at[side, k],
            line_recv.at[side, slot], {"probe": line_slot(k)},
        )

    def pair(slot, k, at):
        return send(
            halo_ref.at[slot], halo_ref.at[slot], pair_send.at[k], pair_recv.at[at], partner
        )

    for side in range(2):

        @pl.when(comes[side])
        def _():
            cross(side).wait_recv()

        @pl.when(jnp.logical_not(comes[side]))
        def _():
            fill = pltpu.make_async_copy(
                (up_ref, down_ref)[side], halo_ref.at[me, side], cross_recv.at[side]
            )
            fill.start()
            fill.wait()

        for k in range(1, CHIPS):
            line(side, me, k).start()
    pair(me, 0, chip).start()
    for k in range(1, CHIPS):
        slot = line_slot(k)
        for side in range(2):
            line(side, slot, k).wait_recv()
        pair(slot, k, lax.div(slot, 2)).start()
    for k in range(CHIPS):
        from_chip = lax.rem(chip + k, CHIPS)
        pair(from_chip * 2 + 1 - core, k, from_chip).wait_recv()
    for side in range(2):

        @pl.when(goes[side])
        def _():
            cross(side).wait_send()

        for k in range(1, CHIPS):
            line(side, me, k).wait_send()
    for k in range(CHIPS):
        pair(me, k, chip).wait_send()


def exchange_halo(up_share, down_share):
    vmem = pl.BlockSpec(memory_space=pltpu.VMEM)
    dma = pltpu.SemaphoreType.DMA
    return pl.pallas_call(
        halo_kernel,
        out_shape=jax.ShapeDtypeStruct((2 * CHIPS, 2) + up_share.shape, jnp.float32),
        in_specs=[vmem, vmem],
        out_specs=pl.BlockSpec(memory_space=pl.ANY),
        scratch_shapes=[
            dma((2,)), dma((2,)), dma((2, CHIPS)), dma((2, 2 * CHIPS)), dma((CHIPS,)),
            dma((CHIPS,)),
        ],
        compiler_params=pltpu.CompilerParams(collective_id=1, has_side_effects=True),
    )(up_share, down_share)


def shards(probe_dirs, log_param, background, site_class, trap_density):
    probe_count, planes, plane_cells = probe_dirs.shape
    slabs, slab = lax.axis_size("space"), lax.axis_index("space")
    up = [(i, i + 1) for i in range(slabs - 1)]
    down = [(j, i) for i, j in up]
    density = jnp.zeros(site_class.shape, jnp.float32)
    for class_index in range(trap_density.shape[0]):
        density = density + jnp.where(site_class == class_index, trap_density[class_index], 0.0)
    trap_rate = density * prolong(jnp.exp(log_param))
    source = -TIME_STEP * trap_rate * background

    def my_share(part):
        both = jnp.concatenate([trap_rate[part], source[part]], axis=0)
        rows = both.reshape((-1, PX * REF))
        length = rows.shape[0] // lax.axis_size("probe")
        return lax.dynamic_slice_in_dim(rows, lax.axis_index("probe") * length, length, 0)

    halo = exchange_halo(my_share(slice(REF - REACH, REF)), my_share(slice(0, REACH)))
    dirs = jnp.concatenate(
        [
            lax.ppermute(probe_dirs, "space", up),
            probe_dirs,
            lax.ppermute(probe_dirs, "space", down),
        ],
        axis=1,
    ).reshape((probe_count, 3, PY, PX))
    edge = jnp.stack([slab > 0, slab < slabs - 1]).astype(jnp.float32)
    images = window_images(edge, trap_rate, source, halo, dirs)
    images = images.reshape((probe_count, planes * plane_cells))
    cell_count = float(planes * slabs * plane_cells)
    q_local, lower_factor = orthogonalize(images, cell_count)
    return (q_local.reshape((probe_count, planes, plane_cells)), lower_factor)


def solution(mesh):
    placed = (
        P("probe", "space", None),
        P("space", None),
        P("space", None, None),
        P("space", None, None),
        P(),
    )
    return jax.shard_map(
        shards,
        mesh=mesh,
        in_specs=placed,
        out_specs=(P("probe", "space", None), P()),
        check_vma=False,
    )
```

```python
import jax
import jax.numpy as jnp
from jax import lax
from jax.experimental import pallas as pl
from jax.experimental.pallas import tpu as pltpu
from jax.sharding import PartitionSpec as P

PX = 64
PY = 4
REF = 8
STEPS = 4


TIME_STEP = 0.12


def prolong(coarse):
    leading = coarse.shape[:-2]
    planes = coarse.shape[-2]
    coarse_grid = coarse.reshape(leading + (planes, PY, PX))
    expanded = jnp.broadcast_to(
        coarse_grid[..., :, None, :, None, :, None], leading + (planes, REF, PY, REF, PX, REF)
    )
    return expanded.reshape(leading + (planes * REF, PY * REF, PX * REF))


def dot_highest(a, b, contract):
    return lax.dot_general(
        a, b, (contract, ((), ())), precision=lax.Precision.HIGHEST,
        preferred_element_type=jnp.float32,
    )


def factor_and_inverse(gram):
    n = gram.shape[0]
    row_at = lax.broadcasted_iota(jnp.int32, (n, 2 * n), 0)
    lane_at = lax.broadcasted_iota(jnp.int32, (n, 2 * n), 1)
    factor_row = lax.broadcasted_iota(jnp.int32, (n, n), 0)
    factor_lane = lax.broadcasted_iota(jnp.int32, (n, n), 1)
    work = jnp.concatenate([gram, jnp.zeros((n, n), jnp.float32)], axis=1)
    work = work + jnp.where(lane_at == row_at + n, 1.0, 0.0)
    factor = jnp.zeros((n, n), jnp.float32)
    for j in range(n):
        scale = lax.rsqrt(work[j : j + 1, j : j + 1])
        row = work[j : j + 1, :] * scale
        column = work[:, j : j + 1] * scale
        keep = (factor_lane == j) & (factor_row >= j)
        factor = jnp.where(keep, jnp.broadcast_to(column, (n, n)), factor)
        work = jnp.where(
            row_at > j, work - column * row, jnp.where(row_at == j, row, work)
        )
    return factor, work[:, n:]


GROUP = 8


def orthogonalize_kernel(
    cell_count, images_ref, q_ref, lower_ref, gathered, rows, grams, image_send, image_recv,
    gram_send, gram_recv,
):
    mesh_id = pl.DeviceIdType.MESH
    me = lax.axis_index("probe")
    place = lax.axis_index("space")
    inner, outer = lax.rem(place, GROUP), lax.div(place, GROUP)

    def probe_peer(k):
        return {"probe": lax.rem(me + k, GROUP)}

    def inner_peer(k):
        return {"space": outer * GROUP + lax.rem(inner + k, GROUP)}

    def outer_peer(k):
        return {"space": lax.rem(outer + k, GROUP) * GROUP + inner}

    barrier = pltpu.get_barrier_semaphore()
    for peer in (probe_peer, inner_peer, outer_peer):
        for k in range(1, GROUP):
            pl.semaphore_signal(barrier, inc=1, device_id=peer(k), device_id_type=mesh_id)
    pl.semaphore_wait(barrier, 3 * (GROUP - 1))

    def send(src, dst, send_sem, recv_sem, device):
        return pltpu.make_async_remote_copy(
            src_ref=src, dst_ref=dst, send_sem=send_sem, recv_sem=recv_sem,
            device_id=device, device_id_type=mesh_id,
        )

    copies = []
    for k in range(1, GROUP):
        copy = send(
            images_ref, gathered.at[me], image_send.at[k], image_recv.at[me], probe_peer(k)
        )
        copy.start()
        copies.append(copy)
    gathered[me] = images_ref[...]
    for k in range(1, GROUP):
        slot = lax.rem(me + k, GROUP)
        send(
            images_ref, gathered.at[slot], image_send.at[k], image_recv.at[slot], probe_peer(k)
        ).wait_recv()
    count = images_ref.shape[0]
    for slot in range(GROUP):
        rows[slot * count : (slot + 1) * count, :] = gathered[slot]

    def group_sum(value, stage, mine, peer):
        box = grams.at[stage]
        box[mine] = value
        for k in range(1, GROUP):
            copy = send(
                box.at[mine], box.at[mine], gram_send.at[stage, k], gram_recv.at[stage, mine],
                peer(k),
            )
            copy.start()
            copies.append(copy)
        for k in range(1, GROUP):
            slot = lax.rem(mine + k, GROUP)
            send(
                box.at[slot], box.at[slot], gram_send.at[stage, k], gram_recv.at[stage, slot],
                peer(k),
            ).wait_recv()
        total = box[0]
        for slot in range(1, GROUP):
            total = total + box[slot]
        return total

    def space_gram(basis, stage):
        gram = dot_highest(basis, basis, ((1,), (1,)))
        gram = group_sum(gram, stage, inner, inner_peer)
        gram = group_sum(gram, stage + 1, outer, outer_peer)
        return gram * (1.0 / cell_count)

    images = rows[...]
    factor_one, inverse_one = factor_and_inverse(space_gram(images, 0))
    basis_one = dot_highest(inverse_one, images, ((1,), (0,)))
    factor_two, inverse_two = factor_and_inverse(space_gram(basis_one, 2))
    q_rows = dot_highest(inverse_two, basis_one, ((1,), (0,)))
    for slot in range(GROUP):
        gathered[slot] = q_rows[slot * count : (slot + 1) * count, :]
    q_ref[...] = gathered[me]
    lower_ref[...] = dot_highest(factor_one, factor_two, ((1,), (0,)))
    for copy in copies:
        copy.wait_send()


def orthogonalize(images, cell_count):
    count, cells = images.shape
    probes = count * GROUP
    vmem = pl.BlockSpec(memory_space=pltpu.VMEM)

    def body(*refs):
        orthogonalize_kernel(cell_count, *refs)

    return pl.pallas_call(
        body,
        out_shape=(
            jax.ShapeDtypeStruct((count, cells), jnp.float32),
            jax.ShapeDtypeStruct((probes, probes), jnp.float32),
        ),
        in_specs=[vmem],
        out_specs=(vmem, vmem),
        scratch_shapes=[
            pltpu.VMEM((GROUP, count, cells), jnp.float32),
            pltpu.VMEM((probes, cells), jnp.float32),
            pltpu.VMEM((4, GROUP, probes, probes), jnp.float32),
            pltpu.SemaphoreType.DMA((GROUP,)),
            pltpu.SemaphoreType.DMA((GROUP,)),
            pltpu.SemaphoreType.DMA((4, GROUP)),
            pltpu.SemaphoreType.DMA((4, GROUP)),
        ],
        compiler_params=pltpu.CompilerParams(collective_id=0, has_side_effects=True),
    )(images)


REACH = 2 * (STEPS - 1)
EXTENDED = REF + 2 * REACH
CHUNK = 16


def window_kernel(
    edge_ref, trap_ref, source_ref, halo_ref, dirs_ref, images_ref, keep, source, first, second,
    summed, wide, narrow,
):
    fine_y, fine_x = PY * REF, PX * REF
    share = halo_ref.shape[2] // CHUNK
    own = slice(REACH, REACH + REF)
    keep[own] = (1.0 - 6.0 * TIME_STEP) - TIME_STEP * trap_ref[...]
    source[own] = source_ref[...]
    for side in range(2):
        base = side * (REACH + REF)
        inside = edge_ref[side]
        for plane in range(REACH):
            for half in range(fine_y // CHUNK):
                rows = slice(half * CHUNK, (half + 1) * CHUNK)

                def piece(at):
                    chunk = at * (fine_y // CHUNK) + half
                    start = (chunk % share) * CHUNK
                    return halo_ref[chunk // share, side, start : start + CHUNK, :]

                trap = piece(plane)
                keep[base + plane, rows, :] = inside * (
                    (1.0 - 6.0 * TIME_STEP) - TIME_STEP * trap
                )
                source[base + plane, rows, :] = inside * piece(REACH + plane)

    x_fine = lax.broadcasted_iota(jnp.int32, (PX, fine_x), 1)
    x_cell = lax.broadcasted_iota(jnp.int32, (PX, fine_x), 0)
    spread_x = jnp.where(x_fine // REF == x_cell, 1.0, 0.0)
    probes = dirs_ref.shape[0]
    all_wide = dot_highest(dirs_ref[...].reshape((-1, PX)), spread_x, ((1,), (0,)))
    for at in range(3 * PY * probes):
        wide[at // PY, at % PY, :] = all_wide[at]
    row_at = lax.broadcasted_iota(jnp.int32, (fine_y, fine_x), 0)
    lane_at = lax.broadcasted_iota(jnp.int32, (fine_y, fine_x), 1)

    def advance(src, dst, low, high, add):
        def plane_step(i, carry):
            below = (i >= REACH).astype(jnp.float32)
            above = (i < REACH + REF).astype(jnp.float32)
            weight = TIME_STEP * (below + (1.0 - below) * edge_ref[0])
            weight = weight * (above + (1.0 - above) * edge_ref[1])
            v = src[i]
            around = src[i - 1] + src[i + 1]
            around += jnp.where(row_at == 0, 0.0, pltpu.roll(v, 1, 0))
            around += jnp.where(row_at == fine_y - 1, 0.0, pltpu.roll(v, fine_y - 1, 0))
            around += jnp.where(lane_at == 0, 0.0, pltpu.roll(v, 1, 1))
            around += jnp.where(lane_at == fine_x - 1, 0.0, pltpu.roll(v, fine_x - 1, 1))
            new = keep[i] * v + weight * around
            dst[i] = new
            if add:
                summed[i] = summed[i] + new
            return carry

        lax.fori_loop(low, high, plane_step, 0, unroll=2)

    def probe_step(p, carry):
        for cell in range(3):
            coarse = wide[3 * p + cell]
            fine = jnp.concatenate(
                [jnp.broadcast_to(coarse[y : y + 1], (REF, fine_x)) for y in range(PY)], axis=0
            )
            low = max(0, REACH - REF + cell * REF)
            high = min(EXTENDED, REACH + cell * REF)
            for i in range(low, high):
                first[i] = source[i] * fine
        bufs = (first, second)
        for n in range(1, 2 * STEPS - 1):
            src, dst = bufs[(n - 1) % 2], bufs[n % 2]
            advance(src, dst, n, EXTENDED - n, n >= STEPS)
            if n == STEPS - 1:
                summed[own] = dst[own]
        total = source[REACH] * summed[REACH]
        for at in range(REACH + 1, REACH + REF):
            total = total + source[at] * summed[at]
        for y in range(PY):
            narrow[p, y : y + 1, :] = jnp.sum(
                total[y * REF : (y + 1) * REF], axis=0, keepdims=True
            )
        return carry

    lax.fori_loop(0, probes, probe_step, 0)
    for p in range(probes):
        images_ref[p] = dot_highest(narrow[p], spread_x, ((1,), (1,)))


def window_images(edge, trap_rate, source, halo, dirs):
    vmem = pl.BlockSpec(memory_space=pltpu.VMEM)
    plane = (PY * REF, PX * REF)
    return pl.pallas_call(
        window_kernel,
        out_shape=jax.ShapeDtypeStruct((dirs.shape[0], PY, PX), jnp.float32),
        in_specs=[pl.BlockSpec(memory_space=pltpu.SMEM)] + [vmem] * 4,
        out_specs=vmem,
        scratch_shapes=[
            pltpu.VMEM((EXTENDED,) + plane, jnp.float32),
            pltpu.VMEM((EXTENDED,) + plane, jnp.float32),
            pltpu.VMEM((EXTENDED,) + plane, jnp.float32),
            pltpu.VMEM((EXTENDED,) + plane, jnp.float32),
            pltpu.VMEM((EXTENDED,) + plane, jnp.float32),
            pltpu.VMEM((3 * dirs.shape[0], PY, PX * REF), jnp.float32),
            pltpu.VMEM((dirs.shape[0], PY, PX * REF), jnp.float32),
        ],
        compiler_params=pltpu.CompilerParams(vmem_limit_bytes=32 * 1024 * 1024),
    )(edge, trap_rate, source, halo, dirs)


CHIPS = 4


def halo_kernel(
    up_ref, down_ref, own_dirs_ref, halo_ref, dirs_ref, cross_send, cross_recv, line_send,
    line_recv, pair_send, pair_recv, dirs_send, dirs_recv,
):
    mesh_id = pl.DeviceIdType.MESH
    me = lax.axis_index("probe")
    slab, slabs = lax.axis_index("space"), lax.axis_size("space")
    core, chip = lax.rem(me, 2), lax.div(me, 2)
    partner = {"probe": chip * 2 + 1 - core}
    has_below, has_above = slab > 0, slab < slabs - 1

    def line_slot(k):
        return lax.rem(chip + k, CHIPS) * 2 + core

    barrier = pltpu.get_barrier_semaphore()

    def greet(device):
        pl.semaphore_signal(barrier, inc=1, device_id=device, device_id_type=mesh_id)

    for k in range(1, CHIPS):
        greet({"probe": line_slot(k)})
    greet(partner)

    @pl.when(has_below)
    def _():
        greet({"space": slab - 1})

    @pl.when(has_above)
    def _():
        greet({"space": slab + 1})

    pl.semaphore_wait(
        barrier, CHIPS + has_below.astype(jnp.int32) + has_above.astype(jnp.int32)
    )

    def send(src, dst, send_sem, recv_sem, device):
        return pltpu.make_async_remote_copy(
            src_ref=src, dst_ref=dst, send_sem=send_sem, recv_sem=recv_sem,
            device_id=device, device_id_type=mesh_id,
        )

    def cross(side):
        share, step = ((up_ref, 1), (down_ref, -1))[side]
        return send(
            share, halo_ref.at[me, side], cross_send.at[side], cross_recv.at[side],
            {"space": slab + step},
        )

    def cross_dirs(side):
        return send(
            own_dirs_ref, dirs_ref.at[side], dirs_send.at[side], dirs_recv.at[side],
            {"space": slab + (1, -1)[side]},
        )

    goes, comes = (has_above, has_below), (has_below, has_above)
    for side in range(2):

        @pl.when(goes[side])
        def _():
            cross(side).start()
            cross_dirs(side).start()

    def line(side, slot, k):
        return send(
            halo_ref.at[slot, side], halo_ref.at[slot, side], line_send.at[side, k],
            line_recv.at[side, slot], {"probe": line_slot(k)},
        )

    def pair(slot, k, at):
        return send(
            halo_ref.at[slot], halo_ref.at[slot], pair_send.at[k], pair_recv.at[at], partner
        )

    for side in range(2):

        @pl.when(comes[side])
        def _():
            cross(side).wait_recv()

        @pl.when(jnp.logical_not(comes[side]))
        def _():
            fill = pltpu.make_async_copy(
                (up_ref, down_ref)[side], halo_ref.at[me, side], cross_recv.at[side]
            )
            fill.start()
            fill.wait()
            fill_dirs = pltpu.make_async_copy(own_dirs_ref, dirs_ref.at[side], dirs_recv.at[side])
            fill_dirs.start()
            fill_dirs.wait()

        for k in range(1, CHIPS):
            line(side, me, k).start()
    pair(me, 0, chip).start()
    for k in range(1, CHIPS):
        slot = line_slot(k)
        for side in range(2):
            line(side, slot, k).wait_recv()
        pair(slot, k, lax.div(slot, 2)).start()
    for k in range(CHIPS):
        from_chip = lax.rem(chip + k, CHIPS)
        pair(from_chip * 2 + 1 - core, k, from_chip).wait_recv()
    for side in range(2):

        @pl.when(comes[side])
        def _():
            cross_dirs(side).wait_recv()

        @pl.when(goes[side])
        def _():
            cross(side).wait_send()
            cross_dirs(side).wait_send()

        for k in range(1, CHIPS):
            line(side, me, k).wait_send()
    for k in range(CHIPS):
        pair(me, k, chip).wait_send()


def exchange_halo(up_share, down_share, own_dirs):
    vmem = pl.BlockSpec(memory_space=pltpu.VMEM)
    dma = pltpu.SemaphoreType.DMA
    return pl.pallas_call(
        halo_kernel,
        out_shape=(
            jax.ShapeDtypeStruct((2 * CHIPS, 2) + up_share.shape, jnp.float32),
            jax.ShapeDtypeStruct((2,) + own_dirs.shape, jnp.float32),
        ),
        in_specs=[vmem, vmem, vmem],
        out_specs=(pl.BlockSpec(memory_space=pl.ANY), pl.BlockSpec(memory_space=pl.ANY)),
        scratch_shapes=[
            dma((2,)), dma((2,)), dma((2, CHIPS)), dma((2, 2 * CHIPS)), dma((CHIPS,)),
            dma((CHIPS,)), dma((2,)), dma((2,)),
        ],
        compiler_params=pltpu.CompilerParams(collective_id=1, has_side_effects=True),
    )(up_share, down_share, own_dirs)


def shards(probe_dirs, log_param, background, site_class, trap_density):
    probe_count, planes, plane_cells = probe_dirs.shape
    slabs, slab = lax.axis_size("space"), lax.axis_index("space")
    density = jnp.zeros(site_class.shape, jnp.float32)
    for class_index in range(trap_density.shape[0]):
        density = density + jnp.where(site_class == class_index, trap_density[class_index], 0.0)
    trap_rate = density * prolong(jnp.exp(log_param))
    source = -TIME_STEP * trap_rate * background

    def my_share(part):
        both = jnp.concatenate([trap_rate[part], source[part]], axis=0)
        rows = both.reshape((-1, PX * REF))
        length = rows.shape[0] // lax.axis_size("probe")
        return lax.dynamic_slice_in_dim(rows, lax.axis_index("probe") * length, length, 0)

    own_dirs = probe_dirs.reshape((probe_count, plane_cells))
    halo, near = exchange_halo(
        my_share(slice(REF - REACH, REF)), my_share(slice(0, REACH)), own_dirs
    )
    dirs = jnp.stack([near[0], own_dirs, near[1]], axis=1).reshape((probe_count, 3, PY, PX))
    edge = jnp.stack([slab > 0, slab < slabs - 1]).astype(jnp.float32)
    images = window_images(edge, trap_rate, source, halo, dirs)
    images = images.reshape((probe_count, planes * plane_cells))
    cell_count = float(planes * slabs * plane_cells)
    q_local, lower_factor = orthogonalize(images, cell_count)
    return (q_local.reshape((probe_count, planes, plane_cells)), lower_factor)


def solution(mesh):
    placed = (
        P("probe", "space", None),
        P("space", None),
        P("space", None, None),
        P("space", None, None),
        P(),
    )
    return jax.shard_map(
        shards,
        mesh=mesh,
        in_specs=placed,
        out_specs=(P("probe", "space", None), P()),
        check_vma=False,
    )
```

```python
import jax
import jax.numpy as jnp
from jax import lax
from jax.experimental import pallas as pl
from jax.experimental.pallas import tpu as pltpu
from jax.sharding import PartitionSpec as P

PX = 64
PY = 4
REF = 8
STEPS = 4


TIME_STEP = 0.12


def prolong(coarse):
    leading = coarse.shape[:-2]
    planes = coarse.shape[-2]
    coarse_grid = coarse.reshape(leading + (planes, PY, PX))
    expanded = jnp.broadcast_to(
        coarse_grid[..., :, None, :, None, :, None], leading + (planes, REF, PY, REF, PX, REF)
    )
    return expanded.reshape(leading + (planes * REF, PY * REF, PX * REF))


def dot_highest(a, b, contract):
    return lax.dot_general(
        a, b, (contract, ((), ())), precision=lax.Precision.HIGHEST,
        preferred_element_type=jnp.float32,
    )


def factor_and_inverse(gram):
    n = gram.shape[0]
    row_at = lax.broadcasted_iota(jnp.int32, (n, 2 * n), 0)
    lane_at = lax.broadcasted_iota(jnp.int32, (n, 2 * n), 1)
    factor_row = lax.broadcasted_iota(jnp.int32, (n, n), 0)
    factor_lane = lax.broadcasted_iota(jnp.int32, (n, n), 1)
    work = jnp.concatenate([gram, jnp.zeros((n, n), jnp.float32)], axis=1)
    work = work + jnp.where(lane_at == row_at + n, 1.0, 0.0)
    factor = jnp.zeros((n, n), jnp.float32)
    for j in range(n):
        scale = lax.rsqrt(work[j : j + 1, j : j + 1])
        row = work[j : j + 1, :] * scale
        column = work[:, j : j + 1] * scale
        keep = (factor_lane == j) & (factor_row >= j)
        factor = jnp.where(keep, jnp.broadcast_to(column, (n, n)), factor)
        work = jnp.where(
            row_at > j, work - column * row, jnp.where(row_at == j, row, work)
        )
    return factor, work[:, n:]


GROUP = 8


def orthogonalize_kernel(
    cell_count, images_ref, q_ref, lower_ref, gathered, rows, grams, image_send, image_recv,
    gram_send, gram_recv,
):
    mesh_id = pl.DeviceIdType.MESH
    me = lax.axis_index("probe")
    place = lax.axis_index("space")
    inner, outer = lax.rem(place, GROUP), lax.div(place, GROUP)

    def probe_peer(k):
        return {"probe": lax.rem(me + k, GROUP)}

    def inner_peer(k):
        return {"space": outer * GROUP + lax.rem(inner + k, GROUP)}

    def outer_peer(k):
        return {"space": lax.rem(outer + k, GROUP) * GROUP + inner}

    barrier = pltpu.get_barrier_semaphore()
    for peer in (probe_peer, inner_peer, outer_peer):
        for k in range(1, GROUP):
            pl.semaphore_signal(barrier, inc=1, device_id=peer(k), device_id_type=mesh_id)
    pl.semaphore_wait(barrier, 3 * (GROUP - 1))

    def send(src, dst, send_sem, recv_sem, device):
        return pltpu.make_async_remote_copy(
            src_ref=src, dst_ref=dst, send_sem=send_sem, recv_sem=recv_sem,
            device_id=device, device_id_type=mesh_id,
        )

    copies = []
    for k in range(1, GROUP):
        copy = send(
            images_ref, gathered.at[me], image_send.at[k], image_recv.at[me], probe_peer(k)
        )
        copy.start()
        copies.append(copy)
    gathered[me] = images_ref[...]
    for k in range(1, GROUP):
        slot = lax.rem(me + k, GROUP)
        send(
            images_ref, gathered.at[slot], image_send.at[k], image_recv.at[slot], probe_peer(k)
        ).wait_recv()
    count = images_ref.shape[0]
    for slot in range(GROUP):
        rows[slot * count : (slot + 1) * count, :] = gathered[slot]

    def group_sum(value, stage, mine, peer):
        box = grams.at[stage]
        box[mine] = value
        for k in range(1, GROUP):
            copy = send(
                box.at[mine], box.at[mine], gram_send.at[stage, k], gram_recv.at[stage, mine],
                peer(k),
            )
            copy.start()
            copies.append(copy)
        for k in range(1, GROUP):
            slot = lax.rem(mine + k, GROUP)
            send(
                box.at[slot], box.at[slot], gram_send.at[stage, k], gram_recv.at[stage, slot],
                peer(k),
            ).wait_recv()
        total = box[0]
        for slot in range(1, GROUP):
            total = total + box[slot]
        return total

    def space_gram(basis, stage):
        gram = dot_highest(basis, basis, ((1,), (1,)))
        gram = group_sum(gram, stage, inner, inner_peer)
        gram = group_sum(gram, stage + 1, outer, outer_peer)
        return gram * (1.0 / cell_count)

    images = rows[...]
    factor_one, inverse_one = factor_and_inverse(space_gram(images, 0))
    basis_one = dot_highest(inverse_one, images, ((1,), (0,)))
    factor_two, inverse_two = factor_and_inverse(space_gram(basis_one, 2))
    q_rows = dot_highest(inverse_two, basis_one, ((1,), (0,)))
    for slot in range(GROUP):
        gathered[slot] = q_rows[slot * count : (slot + 1) * count, :]
    q_ref[...] = gathered[me]
    lower_ref[...] = dot_highest(factor_one, factor_two, ((1,), (0,)))
    for copy in copies:
        copy.wait_send()


def orthogonalize(images, cell_count):
    count, cells = images.shape
    probes = count * GROUP
    vmem = pl.BlockSpec(memory_space=pltpu.VMEM)

    def body(*refs):
        orthogonalize_kernel(cell_count, *refs)

    return pl.pallas_call(
        body,
        out_shape=(
            jax.ShapeDtypeStruct((count, cells), jnp.float32),
            jax.ShapeDtypeStruct((probes, probes), jnp.float32),
        ),
        in_specs=[vmem],
        out_specs=(vmem, vmem),
        scratch_shapes=[
            pltpu.VMEM((GROUP, count, cells), jnp.float32),
            pltpu.VMEM((probes, cells), jnp.float32),
            pltpu.VMEM((4, GROUP, probes, probes), jnp.float32),
            pltpu.SemaphoreType.DMA((GROUP,)),
            pltpu.SemaphoreType.DMA((GROUP,)),
            pltpu.SemaphoreType.DMA((4, GROUP)),
            pltpu.SemaphoreType.DMA((4, GROUP)),
        ],
        compiler_params=pltpu.CompilerParams(collective_id=0, has_side_effects=True),
    )(images)


REACH = 2 * (STEPS - 1)
EXTENDED = REF + 2 * REACH
CHUNK = 16


def window_kernel(
    edge_ref, trap_ref, source_ref, halo_ref, dirs_ref, images_ref, keep, source, first, second,
    summed, wide, narrow,
):
    fine_y, fine_x = PY * REF, PX * REF
    share = halo_ref.shape[2] // CHUNK
    own = slice(REACH, REACH + REF)
    keep[own] = (1.0 - 6.0 * TIME_STEP) - TIME_STEP * trap_ref[...]
    source[own] = source_ref[...]
    for side in range(2):
        base = side * (REACH + REF)
        inside = edge_ref[side]
        for plane in range(REACH):
            for half in range(fine_y // CHUNK):
                rows = slice(half * CHUNK, (half + 1) * CHUNK)

                def piece(at):
                    chunk = at * (fine_y // CHUNK) + half
                    start = (chunk % share) * CHUNK
                    return halo_ref[chunk // share, side, start : start + CHUNK, :]

                trap = piece(plane)
                keep[base + plane, rows, :] = inside * (
                    (1.0 - 6.0 * TIME_STEP) - TIME_STEP * trap
                )
                source[base + plane, rows, :] = inside * piece(REACH + plane)

    x_fine = lax.broadcasted_iota(jnp.int32, (PX, fine_x), 1)
    x_cell = lax.broadcasted_iota(jnp.int32, (PX, fine_x), 0)
    spread_x = jnp.where(x_fine // REF == x_cell, 1.0, 0.0)
    probes = dirs_ref.shape[0]
    all_wide = dot_highest(dirs_ref[...].reshape((-1, PX)), spread_x, ((1,), (0,)))
    for at in range(3 * PY * probes):
        wide[at // PY, at % PY, :] = all_wide[at]
    row_at = lax.broadcasted_iota(jnp.int32, (fine_y, fine_x), 0)
    lane_at = lax.broadcasted_iota(jnp.int32, (fine_y, fine_x), 1)

    def advance(src, dst, low, high, add):
        for i in range(low, high):
            weight = TIME_STEP
            if i < REACH:
                weight = TIME_STEP * edge_ref[0]
            elif i >= REACH + REF:
                weight = TIME_STEP * edge_ref[1]
            v = src[i]
            around = src[i - 1] + src[i + 1]
            around += jnp.where(row_at == 0, 0.0, pltpu.roll(v, 1, 0))
            around += jnp.where(row_at == fine_y - 1, 0.0, pltpu.roll(v, fine_y - 1, 0))
            around += jnp.where(lane_at == 0, 0.0, pltpu.roll(v, 1, 1))
            around += jnp.where(lane_at == fine_x - 1, 0.0, pltpu.roll(v, fine_x - 1, 1))
            new = keep[i] * v + weight * around
            dst[i] = new
            if add and REACH <= i < REACH + REF:
                summed[i] = summed[i] + new

    def probe_step(p, carry):
        for cell in range(3):
            coarse = wide[3 * p + cell]
            fine = jnp.concatenate(
                [jnp.broadcast_to(coarse[y : y + 1], (REF, fine_x)) for y in range(PY)], axis=0
            )
            low = max(0, REACH - REF + cell * REF)
            high = min(EXTENDED, REACH + cell * REF)
            for i in range(low, high):
                first[i] = source[i] * fine
        bufs = (first, second)
        for n in range(1, 2 * STEPS - 1):
            src, dst = bufs[(n - 1) % 2], bufs[n % 2]
            advance(src, dst, n, EXTENDED - n, n >= STEPS)
            if n == STEPS - 1:
                summed[own] = dst[own]
        total = source[REACH] * summed[REACH]
        for at in range(REACH + 1, REACH + REF):
            total = total + source[at] * summed[at]
        for y in range(PY):
            narrow[p, y : y + 1, :] = jnp.sum(
                total[y * REF : (y + 1) * REF], axis=0, keepdims=True
            )
        return carry

    lax.fori_loop(0, probes, probe_step, 0)
    for p in range(probes):
        images_ref[p] = dot_highest(narrow[p], spread_x, ((1,), (1,)))


def window_images(edge, trap_rate, source, halo, dirs):
    vmem = pl.BlockSpec(memory_space=pltpu.VMEM)
    plane = (PY * REF, PX * REF)
    return pl.pallas_call(
        window_kernel,
        out_shape=jax.ShapeDtypeStruct((dirs.shape[0], PY, PX), jnp.float32),
        in_specs=[pl.BlockSpec(memory_space=pltpu.SMEM)] + [vmem] * 4,
        out_specs=vmem,
        scratch_shapes=[
            pltpu.VMEM((EXTENDED,) + plane, jnp.float32),
            pltpu.VMEM((EXTENDED,) + plane, jnp.float32),
            pltpu.VMEM((EXTENDED,) + plane, jnp.float32),
            pltpu.VMEM((EXTENDED,) + plane, jnp.float32),
            pltpu.VMEM((EXTENDED,) + plane, jnp.float32),
            pltpu.VMEM((3 * dirs.shape[0], PY, PX * REF), jnp.float32),
            pltpu.VMEM((dirs.shape[0], PY, PX * REF), jnp.float32),
        ],
        compiler_params=pltpu.CompilerParams(vmem_limit_bytes=32 * 1024 * 1024),
    )(edge, trap_rate, source, halo, dirs)


CHIPS = 4


def halo_kernel(
    up_ref, down_ref, own_dirs_ref, halo_ref, dirs_ref, cross_send, cross_recv, line_send,
    line_recv, pair_send, pair_recv, dirs_send, dirs_recv,
):
    mesh_id = pl.DeviceIdType.MESH
    me = lax.axis_index("probe")
    slab, slabs = lax.axis_index("space"), lax.axis_size("space")
    core, chip = lax.rem(me, 2), lax.div(me, 2)
    partner = {"probe": chip * 2 + 1 - core}
    has_below, has_above = slab > 0, slab < slabs - 1

    def line_slot(k):
        return lax.rem(chip + k, CHIPS) * 2 + core

    barrier = pltpu.get_barrier_semaphore()

    def greet(device):
        pl.semaphore_signal(barrier, inc=1, device_id=device, device_id_type=mesh_id)

    for k in range(1, CHIPS):
        greet({"probe": line_slot(k)})
    greet(partner)

    @pl.when(has_below)
    def _():
        greet({"space": slab - 1})

    @pl.when(has_above)
    def _():
        greet({"space": slab + 1})

    pl.semaphore_wait(
        barrier, CHIPS + has_below.astype(jnp.int32) + has_above.astype(jnp.int32)
    )

    def send(src, dst, send_sem, recv_sem, device):
        return pltpu.make_async_remote_copy(
            src_ref=src, dst_ref=dst, send_sem=send_sem, recv_sem=recv_sem,
            device_id=device, device_id_type=mesh_id,
        )

    def cross(side):
        share, step = ((up_ref, 1), (down_ref, -1))[side]
        return send(
            share, halo_ref.at[me, side], cross_send.at[side], cross_recv.at[side],
            {"space": slab + step},
        )

    def cross_dirs(side):
        return send(
            own_dirs_ref, dirs_ref.at[side], dirs_send.at[side], dirs_recv.at[side],
            {"space": slab + (1, -1)[side]},
        )

    goes, comes = (has_above, has_below), (has_below, has_above)
    for side in range(2):

        @pl.when(goes[side])
        def _():
            cross(side).start()
            cross_dirs(side).start()

    def line(side, slot, k):
        return send(
            halo_ref.at[slot, side], halo_ref.at[slot, side], line_send.at[side, k],
            line_recv.at[side, slot], {"probe": line_slot(k)},
        )

    def pair(slot, k, at):
        return send(
            halo_ref.at[slot], halo_ref.at[slot], pair_send.at[k], pair_recv.at[at], partner
        )

    for side in range(2):

        @pl.when(comes[side])
        def _():
            cross(side).wait_recv()

        @pl.when(jnp.logical_not(comes[side]))
        def _():
            fill = pltpu.make_async_copy(
                (up_ref, down_ref)[side], halo_ref.at[me, side], cross_recv.at[side]
            )
            fill.start()
            fill.wait()
            fill_dirs = pltpu.make_async_copy(own_dirs_ref, dirs_ref.at[side], dirs_recv.at[side])
            fill_dirs.start()
            fill_dirs.wait()

        for k in range(1, CHIPS):
            line(side, me, k).start()
    pair(me, 0, chip).start()
    for k in range(1, CHIPS):
        slot = line_slot(k)
        for side in range(2):
            line(side, slot, k).wait_recv()
        pair(slot, k, lax.div(slot, 2)).start()
    for k in range(CHIPS):
        from_chip = lax.rem(chip + k, CHIPS)
        pair(from_chip * 2 + 1 - core, k, from_chip).wait_recv()
    for side in range(2):

        @pl.when(comes[side])
        def _():
            cross_dirs(side).wait_recv()

        @pl.when(goes[side])
        def _():
            cross(side).wait_send()
            cross_dirs(side).wait_send()

        for k in range(1, CHIPS):
            line(side, me, k).wait_send()
    for k in range(CHIPS):
        pair(me, k, chip).wait_send()


def exchange_halo(up_share, down_share, own_dirs):
    vmem = pl.BlockSpec(memory_space=pltpu.VMEM)
    dma = pltpu.SemaphoreType.DMA
    return pl.pallas_call(
        halo_kernel,
        out_shape=(
            jax.ShapeDtypeStruct((2 * CHIPS, 2) + up_share.shape, jnp.float32),
            jax.ShapeDtypeStruct((2,) + own_dirs.shape, jnp.float32),
        ),
        in_specs=[vmem, vmem, vmem],
        out_specs=(pl.BlockSpec(memory_space=pl.ANY), pl.BlockSpec(memory_space=pl.ANY)),
        scratch_shapes=[
            dma((2,)), dma((2,)), dma((2, CHIPS)), dma((2, 2 * CHIPS)), dma((CHIPS,)),
            dma((CHIPS,)), dma((2,)), dma((2,)),
        ],
        compiler_params=pltpu.CompilerParams(collective_id=1, has_side_effects=True),
    )(up_share, down_share, own_dirs)


def shards(probe_dirs, log_param, background, site_class, trap_density):
    probe_count, planes, plane_cells = probe_dirs.shape
    slabs, slab = lax.axis_size("space"), lax.axis_index("space")
    density = jnp.zeros(site_class.shape, jnp.float32)
    for class_index in range(trap_density.shape[0]):
        density = density + jnp.where(site_class == class_index, trap_density[class_index], 0.0)
    trap_rate = density * prolong(jnp.exp(log_param))
    source = -TIME_STEP * trap_rate * background

    def my_share(part):
        both = jnp.concatenate([trap_rate[part], source[part]], axis=0)
        rows = both.reshape((-1, PX * REF))
        length = rows.shape[0] // lax.axis_size("probe")
        return lax.dynamic_slice_in_dim(rows, lax.axis_index("probe") * length, length, 0)

    own_dirs = probe_dirs.reshape((probe_count, plane_cells))
    halo, near = exchange_halo(
        my_share(slice(REF - REACH, REF)), my_share(slice(0, REACH)), own_dirs
    )
    dirs = jnp.stack([near[0], own_dirs, near[1]], axis=1).reshape((probe_count, 3, PY, PX))
    edge = jnp.stack([slab > 0, slab < slabs - 1]).astype(jnp.float32)
    images = window_images(edge, trap_rate, source, halo, dirs)
    images = images.reshape((probe_count, planes * plane_cells))
    cell_count = float(planes * slabs * plane_cells)
    q_local, lower_factor = orthogonalize(images, cell_count)
    return (q_local.reshape((probe_count, planes, plane_cells)), lower_factor)


def solution(mesh):
    placed = (
        P("probe", "space", None),
        P("space", None),
        P("space", None, None),
        P("space", None, None),
        P(),
    )
    return jax.shard_map(
        shards,
        mesh=mesh,
        in_specs=placed,
        out_specs=(P("probe", "space", None), P()),
        check_vma=False,
    )
```

```python
import jax
import jax.numpy as jnp
from jax import lax
from jax.experimental import pallas as pl
from jax.experimental.pallas import tpu as pltpu
from jax.sharding import PartitionSpec as P

PX = 64
PY = 4
REF = 8
STEPS = 4


TIME_STEP = 0.12


def prolong(coarse):
    leading = coarse.shape[:-2]
    planes = coarse.shape[-2]
    coarse_grid = coarse.reshape(leading + (planes, PY, PX))
    expanded = jnp.broadcast_to(
        coarse_grid[..., :, None, :, None, :, None], leading + (planes, REF, PY, REF, PX, REF)
    )
    return expanded.reshape(leading + (planes * REF, PY * REF, PX * REF))


def dot_highest(a, b, contract):
    return lax.dot_general(
        a, b, (contract, ((), ())), precision=lax.Precision.HIGHEST,
        preferred_element_type=jnp.float32,
    )


def factor_and_inverse(gram):
    n = gram.shape[0]
    row_at = lax.broadcasted_iota(jnp.int32, (n, 2 * n), 0)
    lane_at = lax.broadcasted_iota(jnp.int32, (n, 2 * n), 1)
    factor_row = lax.broadcasted_iota(jnp.int32, (n, n), 0)
    factor_lane = lax.broadcasted_iota(jnp.int32, (n, n), 1)
    work = jnp.concatenate([gram, jnp.zeros((n, n), jnp.float32)], axis=1)
    work = work + jnp.where(lane_at == row_at + n, 1.0, 0.0)
    factor = jnp.zeros((n, n), jnp.float32)
    for j in range(n):
        scale = lax.rsqrt(work[j : j + 1, j : j + 1])
        row = work[j : j + 1, :] * scale
        column = work[:, j : j + 1] * scale
        keep = (factor_lane == j) & (factor_row >= j)
        factor = jnp.where(keep, jnp.broadcast_to(column, (n, n)), factor)
        work = jnp.where(
            row_at > j, work - column * row, jnp.where(row_at == j, row, work)
        )
    return factor, work[:, n:]


GROUP = 8


def orthogonalize_kernel(
    cell_count, images_ref, q_ref, lower_ref, gathered, rows, grams, image_send, image_recv,
    gram_send, gram_recv,
):
    mesh_id = pl.DeviceIdType.MESH
    me = lax.axis_index("probe")
    place = lax.axis_index("space")
    inner, outer = lax.rem(place, GROUP), lax.div(place, GROUP)

    def probe_peer(k):
        return {"probe": lax.rem(me + k, GROUP)}

    def inner_peer(k):
        return {"space": outer * GROUP + lax.rem(inner + k, GROUP)}

    def outer_peer(k):
        return {"space": lax.rem(outer + k, GROUP) * GROUP + inner}

    barrier = pltpu.get_barrier_semaphore()
    for peer in (probe_peer, inner_peer, outer_peer):
        for k in range(1, GROUP):
            pl.semaphore_signal(barrier, inc=1, device_id=peer(k), device_id_type=mesh_id)
    pl.semaphore_wait(barrier, 3 * (GROUP - 1))

    def send(src, dst, send_sem, recv_sem, device):
        return pltpu.make_async_remote_copy(
            src_ref=src, dst_ref=dst, send_sem=send_sem, recv_sem=recv_sem,
            device_id=device, device_id_type=mesh_id,
        )

    copies = []
    for k in range(1, GROUP):
        copy = send(
            images_ref, gathered.at[me], image_send.at[k], image_recv.at[me], probe_peer(k)
        )
        copy.start()
        copies.append(copy)
    gathered[me] = images_ref[...]
    for k in range(1, GROUP):
        slot = lax.rem(me + k, GROUP)
        send(
            images_ref, gathered.at[slot], image_send.at[k], image_recv.at[slot], probe_peer(k)
        ).wait_recv()
    count = images_ref.shape[0]
    for slot in range(GROUP):
        rows[slot * count : (slot + 1) * count, :] = gathered[slot]

    def group_sum(value, stage, mine, peer):
        box = grams.at[stage]
        box[mine] = value
        for k in range(1, GROUP):
            copy = send(
                box.at[mine], box.at[mine], gram_send.at[stage, k], gram_recv.at[stage, mine],
                peer(k),
            )
            copy.start()
            copies.append(copy)
        for k in range(1, GROUP):
            slot = lax.rem(mine + k, GROUP)
            send(
                box.at[slot], box.at[slot], gram_send.at[stage, k], gram_recv.at[stage, slot],
                peer(k),
            ).wait_recv()
        total = box[0]
        for slot in range(1, GROUP):
            total = total + box[slot]
        return total

    def space_gram(basis, stage):
        gram = dot_highest(basis, basis, ((1,), (1,)))
        gram = group_sum(gram, stage, inner, inner_peer)
        gram = group_sum(gram, stage + 1, outer, outer_peer)
        return gram * (1.0 / cell_count)

    images = rows[...]
    factor_one, inverse_one = factor_and_inverse(space_gram(images, 0))
    basis_one = dot_highest(inverse_one, images, ((1,), (0,)))
    factor_two, inverse_two = factor_and_inverse(space_gram(basis_one, 2))
    q_rows = dot_highest(inverse_two, basis_one, ((1,), (0,)))
    for slot in range(GROUP):
        gathered[slot] = q_rows[slot * count : (slot + 1) * count, :]
    q_ref[...] = gathered[me]
    lower_ref[...] = dot_highest(factor_one, factor_two, ((1,), (0,)))
    for copy in copies:
        copy.wait_send()


def orthogonalize(images, cell_count):
    count, cells = images.shape
    probes = count * GROUP
    vmem = pl.BlockSpec(memory_space=pltpu.VMEM)

    def body(*refs):
        orthogonalize_kernel(cell_count, *refs)

    return pl.pallas_call(
        body,
        out_shape=(
            jax.ShapeDtypeStruct((count, cells), jnp.float32),
            jax.ShapeDtypeStruct((probes, probes), jnp.float32),
        ),
        in_specs=[vmem],
        out_specs=(vmem, vmem),
        scratch_shapes=[
            pltpu.VMEM((GROUP, count, cells), jnp.float32),
            pltpu.VMEM((probes, cells), jnp.float32),
            pltpu.VMEM((4, GROUP, probes, probes), jnp.float32),
            pltpu.SemaphoreType.DMA((GROUP,)),
            pltpu.SemaphoreType.DMA((GROUP,)),
            pltpu.SemaphoreType.DMA((4, GROUP)),
            pltpu.SemaphoreType.DMA((4, GROUP)),
        ],
        compiler_params=pltpu.CompilerParams(collective_id=0, has_side_effects=True),
    )(images)


REACH = 2 * (STEPS - 1)
EXTENDED = REF + 2 * REACH
CHUNK = 16


def window_kernel(
    edge_ref, trap_ref, source_ref, halo_ref, dirs_ref, images_ref, keep, source, first, second,
    summed, wide, narrow,
):
    fine_y, fine_x = PY * REF, PX * REF
    share = halo_ref.shape[2] // CHUNK
    own = slice(REACH, REACH + REF)
    keep[own] = (1.0 - 6.0 * TIME_STEP) - TIME_STEP * trap_ref[...]
    source[own] = source_ref[...]
    for side in range(2):
        base = side * (REACH + REF)
        inside = edge_ref[side]
        for plane in range(REACH):
            for half in range(fine_y // CHUNK):
                rows = slice(half * CHUNK, (half + 1) * CHUNK)

                def piece(at):
                    chunk = at * (fine_y // CHUNK) + half
                    start = (chunk % share) * CHUNK
                    return halo_ref[chunk // share, side, start : start + CHUNK, :]

                trap = piece(plane)
                keep[base + plane, rows, :] = inside * (
                    (1.0 - 6.0 * TIME_STEP) - TIME_STEP * trap
                )
                source[base + plane, rows, :] = inside * piece(REACH + plane)

    x_fine = lax.broadcasted_iota(jnp.int32, (PX, fine_x), 1)
    x_cell = lax.broadcasted_iota(jnp.int32, (PX, fine_x), 0)
    spread_x = jnp.where(x_fine // REF == x_cell, 1.0, 0.0)
    probes = dirs_ref.shape[0]
    all_wide = dot_highest(dirs_ref[...].reshape((-1, PX)), spread_x, ((1,), (0,)))
    for at in range(3 * PY * probes):
        wide[at // PY, at % PY, :] = all_wide[at]
    edge_row = jnp.zeros((1, fine_x), jnp.float32)
    lane_at = lax.broadcasted_iota(jnp.int32, (fine_y, fine_x), 1)

    def advance(src, dst, low, high, add):
        for i in range(low, high):
            weight = TIME_STEP
            if i < REACH:
                weight = TIME_STEP * edge_ref[0]
            elif i >= REACH + REF:
                weight = TIME_STEP * edge_ref[1]
            v = src[i]
            around = src[i - 1] + src[i + 1]
            around += jnp.concatenate([edge_row, src[i, : fine_y - 1, :]], axis=0)
            around += jnp.concatenate([src[i, 1:, :], edge_row], axis=0)
            around += jnp.where(lane_at == 0, 0.0, pltpu.roll(v, 1, 1))
            around += jnp.where(lane_at == fine_x - 1, 0.0, pltpu.roll(v, fine_x - 1, 1))
            new = keep[i] * v + weight * around
            dst[i] = new
            if add and REACH <= i < REACH + REF:
                summed[i] = summed[i] + new

    def probe_step(p, carry):
        for cell in range(3):
            coarse = wide[3 * p + cell]
            fine = jnp.concatenate(
                [jnp.broadcast_to(coarse[y : y + 1], (REF, fine_x)) for y in range(PY)], axis=0
            )
            low = max(0, REACH - REF + cell * REF)
            high = min(EXTENDED, REACH + cell * REF)
            for i in range(low, high):
                first[i] = source[i] * fine
        bufs = (first, second)
        for n in range(1, 2 * STEPS - 1):
            src, dst = bufs[(n - 1) % 2], bufs[n % 2]
            advance(src, dst, n, EXTENDED - n, n >= STEPS)
            if n == STEPS - 1:
                summed[own] = dst[own]
        total = source[REACH] * summed[REACH]
        for at in range(REACH + 1, REACH + REF):
            total = total + source[at] * summed[at]
        for y in range(PY):
            narrow[p, y : y + 1, :] = jnp.sum(
                total[y * REF : (y + 1) * REF], axis=0, keepdims=True
            )
        return carry

    lax.fori_loop(0, probes, probe_step, 0)
    for p in range(probes):
        images_ref[p] = dot_highest(narrow[p], spread_x, ((1,), (1,)))


def window_images(edge, trap_rate, source, halo, dirs):
    vmem = pl.BlockSpec(memory_space=pltpu.VMEM)
    plane = (PY * REF, PX * REF)
    return pl.pallas_call(
        window_kernel,
        out_shape=jax.ShapeDtypeStruct((dirs.shape[0], PY, PX), jnp.float32),
        in_specs=[pl.BlockSpec(memory_space=pltpu.SMEM)] + [vmem] * 4,
        out_specs=vmem,
        scratch_shapes=[
            pltpu.VMEM((EXTENDED,) + plane, jnp.float32),
            pltpu.VMEM((EXTENDED,) + plane, jnp.float32),
            pltpu.VMEM((EXTENDED,) + plane, jnp.float32),
            pltpu.VMEM((EXTENDED,) + plane, jnp.float32),
            pltpu.VMEM((EXTENDED,) + plane, jnp.float32),
            pltpu.VMEM((3 * dirs.shape[0], PY, PX * REF), jnp.float32),
            pltpu.VMEM((dirs.shape[0], PY, PX * REF), jnp.float32),
        ],
        compiler_params=pltpu.CompilerParams(vmem_limit_bytes=32 * 1024 * 1024),
    )(edge, trap_rate, source, halo, dirs)


CHIPS = 4


def halo_kernel(
    up_ref, down_ref, own_dirs_ref, halo_ref, dirs_ref, cross_send, cross_recv, line_send,
    line_recv, pair_send, pair_recv, dirs_send, dirs_recv,
):
    mesh_id = pl.DeviceIdType.MESH
    me = lax.axis_index("probe")
    slab, slabs = lax.axis_index("space"), lax.axis_size("space")
    core, chip = lax.rem(me, 2), lax.div(me, 2)
    partner = {"probe": chip * 2 + 1 - core}
    has_below, has_above = slab > 0, slab < slabs - 1

    def line_slot(k):
        return lax.rem(chip + k, CHIPS) * 2 + core

    barrier = pltpu.get_barrier_semaphore()

    def greet(device):
        pl.semaphore_signal(barrier, inc=1, device_id=device, device_id_type=mesh_id)

    for k in range(1, CHIPS):
        greet({"probe": line_slot(k)})
    greet(partner)

    @pl.when(has_below)
    def _():
        greet({"space": slab - 1})

    @pl.when(has_above)
    def _():
        greet({"space": slab + 1})

    pl.semaphore_wait(
        barrier, CHIPS + has_below.astype(jnp.int32) + has_above.astype(jnp.int32)
    )

    def send(src, dst, send_sem, recv_sem, device):
        return pltpu.make_async_remote_copy(
            src_ref=src, dst_ref=dst, send_sem=send_sem, recv_sem=recv_sem,
            device_id=device, device_id_type=mesh_id,
        )

    def cross(side):
        share, step = ((up_ref, 1), (down_ref, -1))[side]
        return send(
            share, halo_ref.at[me, side], cross_send.at[side], cross_recv.at[side],
            {"space": slab + step},
        )

    def cross_dirs(side):
        return send(
            own_dirs_ref, dirs_ref.at[side], dirs_send.at[side], dirs_recv.at[side],
            {"space": slab + (1, -1)[side]},
        )

    goes, comes = (has_above, has_below), (has_below, has_above)
    for side in range(2):

        @pl.when(goes[side])
        def _():
            cross(side).start()
            cross_dirs(side).start()

    def line(side, slot, k):
        return send(
            halo_ref.at[slot, side], halo_ref.at[slot, side], line_send.at[side, k],
            line_recv.at[side, slot], {"probe": line_slot(k)},
        )

    def pair(slot, k, at):
        return send(
            halo_ref.at[slot], halo_ref.at[slot], pair_send.at[k], pair_recv.at[at], partner
        )

    for side in range(2):

        @pl.when(comes[side])
        def _():
            cross(side).wait_recv()

        @pl.when(jnp.logical_not(comes[side]))
        def _():
            fill = pltpu.make_async_copy(
                (up_ref, down_ref)[side], halo_ref.at[me, side], cross_recv.at[side]
            )
            fill.start()
            fill.wait()
            fill_dirs = pltpu.make_async_copy(own_dirs_ref, dirs_ref.at[side], dirs_recv.at[side])
            fill_dirs.start()
            fill_dirs.wait()

        for k in range(1, CHIPS):
            line(side, me, k).start()
    pair(me, 0, chip).start()
    for k in range(1, CHIPS):
        slot = line_slot(k)
        for side in range(2):
            line(side, slot, k).wait_recv()
        pair(slot, k, lax.div(slot, 2)).start()
    for k in range(CHIPS):
        from_chip = lax.rem(chip + k, CHIPS)
        pair(from_chip * 2 + 1 - core, k, from_chip).wait_recv()
    for side in range(2):

        @pl.when(comes[side])
        def _():
            cross_dirs(side).wait_recv()

        @pl.when(goes[side])
        def _():
            cross(side).wait_send()
            cross_dirs(side).wait_send()

        for k in range(1, CHIPS):
            line(side, me, k).wait_send()
    for k in range(CHIPS):
        pair(me, k, chip).wait_send()


def exchange_halo(up_share, down_share, own_dirs):
    vmem = pl.BlockSpec(memory_space=pltpu.VMEM)
    dma = pltpu.SemaphoreType.DMA
    return pl.pallas_call(
        halo_kernel,
        out_shape=(
            jax.ShapeDtypeStruct((2 * CHIPS, 2) + up_share.shape, jnp.float32),
            jax.ShapeDtypeStruct((2,) + own_dirs.shape, jnp.float32),
        ),
        in_specs=[vmem, vmem, vmem],
        out_specs=(pl.BlockSpec(memory_space=pl.ANY), pl.BlockSpec(memory_space=pl.ANY)),
        scratch_shapes=[
            dma((2,)), dma((2,)), dma((2, CHIPS)), dma((2, 2 * CHIPS)), dma((CHIPS,)),
            dma((CHIPS,)), dma((2,)), dma((2,)),
        ],
        compiler_params=pltpu.CompilerParams(collective_id=1, has_side_effects=True),
    )(up_share, down_share, own_dirs)


def shards(probe_dirs, log_param, background, site_class, trap_density):
    probe_count, planes, plane_cells = probe_dirs.shape
    slabs, slab = lax.axis_size("space"), lax.axis_index("space")
    density = jnp.zeros(site_class.shape, jnp.float32)
    for class_index in range(trap_density.shape[0]):
        density = density + jnp.where(site_class == class_index, trap_density[class_index], 0.0)
    trap_rate = density * prolong(jnp.exp(log_param))
    source = -TIME_STEP * trap_rate * background

    def my_share(part):
        both = jnp.concatenate([trap_rate[part], source[part]], axis=0)
        rows = both.reshape((-1, PX * REF))
        length = rows.shape[0] // lax.axis_size("probe")
        return lax.dynamic_slice_in_dim(rows, lax.axis_index("probe") * length, length, 0)

    own_dirs = probe_dirs.reshape((probe_count, plane_cells))
    halo, near = exchange_halo(
        my_share(slice(REF - REACH, REF)), my_share(slice(0, REACH)), own_dirs
    )
    dirs = jnp.stack([near[0], own_dirs, near[1]], axis=1).reshape((probe_count, 3, PY, PX))
    edge = jnp.stack([slab > 0, slab < slabs - 1]).astype(jnp.float32)
    images = window_images(edge, trap_rate, source, halo, dirs)
    images = images.reshape((probe_count, planes * plane_cells))
    cell_count = float(planes * slabs * plane_cells)
    q_local, lower_factor = orthogonalize(images, cell_count)
    return (q_local.reshape((probe_count, planes, plane_cells)), lower_factor)


def solution(mesh):
    placed = (
        P("probe", "space", None),
        P("space", None),
        P("space", None, None),
        P("space", None, None),
        P(),
    )
    return jax.shard_map(
        shards,
        mesh=mesh,
        in_specs=placed,
        out_specs=(P("probe", "space", None), P()),
        check_vma=False,
    )
```
